32 devices in a mesh: comp: 4 (over y, x), dom: 8 (over z, core).
Axes of the slice: x: 2, y: 2, z: 4, core: 2. Of those that a mesh axis runs over, the one named last changes fastest.
Arguments:
- densities: float32 [4, 3072, 2048], P('comp', 'dom'), may hold values from -6 to 6
- levels: int32 [4, 2], P('comp'), may hold values from 0 to 3
- coeffs: int32 [4], P('comp'), may hold values from -1 to 1, as said below
Outputs:
- result: float32 [4, 3072, 2048], P('comp', 'dom')
The draws below stay inside these ranges and needn't reach their ends.
Inputs may be any that keep to these rules, and one draw needn't show every extreme that they name: `coeffs`: each coefficient is -1 or 1; both values occur.
All inputs are finite; a program needn't handle non-finite values.
Results may differ from the reference program's by a relative error of at most 0.0001.
Values sent between devices are 32-bit elements; how exact they have to be, the bound alone decides.
No kernel may reach another device: no remote copies, remote signals or barrier semaphores. Data moves between devices by JAX's collectives and lax.ppermute only.
A program may use at most 64 MiB of HBM per device.

```python
import jax
import jax.numpy as jnp
from jax import lax

NV = 2048
MX = 2048
MV = 256
PRE = 8
POST = 2
GROUPS = 4
NX = 3072


def draw_coeffs(key, part):
    sign_key = jax.random.fold_in(key, 11)
    order_key = jax.random.fold_in(key, 23)
    signs = 2 * jax.random.randint(sign_key, (GROUPS,), 0, 2) - 1
    order = jax.random.permutation(order_key, GROUPS)
    fixed = jnp.where(order == 0, 1, jnp.where(order == 1, -1, signs))
    return fixed.astype(jnp.int32)


def plant(array, key, least, high):
    spot = [jax.random.randint(jax.random.fold_in(key, axis), (), 0, length) for axis, length in enumerate(array.shape)]
    main_axis = array.shape.index(max(array.shape))
    beside = spot[:main_axis] + [(spot[main_axis] + 1) % array.shape[main_axis]] + spot[main_axis + 1:]
    return array.at[tuple(spot)].set(least).at[tuple(beside)].set(high)


def block_scale(own_key, extent, pieces, low, top_value):
    factor_of, own = 1.0, jax.random.fold_in(own_key, 6)
    for axis_at, blocks in pieces:
        steps = jnp.exp(jax.random.uniform(jax.random.fold_in(own, axis_at), (blocks,), jnp.float32, low / len(pieces), top_value / len(pieces)))
        factor_of = factor_of * jnp.repeat(steps, extent[axis_at] // blocks).reshape([-1 if axis == axis_at else 1 for axis in range(len(extent))])
    return factor_of


def scatter_about(key, dims, deviation, limit, shards=(), kind=jnp.bfloat16):
    entries = jax.random.normal(key, dims, jnp.float32) * deviation
    if len(shards) > 0:
        entries = block_scale(key, dims, shards, -0.22, 0.18) * entries
    return jnp.clip(entries, min=-limit, max=limit).astype(kind)


def setup_inputs(seed: int = 0) -> dict:
    streams_of = jax.random.split(jax.random.key(seed), 4)
    return {
        "densities": scatter_about(streams_of[0], (GROUPS, NX, NV), 1.0, 6.0, ((0, 4), (1, 8)), jnp.float32),
        "levels": plant(jax.random.randint(streams_of[1], (GROUPS, 2), 0, 4), jax.random.fold_in(streams_of[1], 1), 0, 3).astype(jnp.int32),
        "coeffs": draw_coeffs(jax.random.fold_in(streams_of[3], 71), 0),
    }


HIGHEST_PRECISION = lax.Precision.HIGHEST

def cosine_basis(positions, mode_count, length):
    mode_ids = jnp.arange(mode_count, dtype=jnp.float32)
    phases = jnp.pi * (positions[:, None] + 0.5) * mode_ids[None, :] / length
    column_scale = jnp.where(mode_ids == 0, jnp.sqrt(1.0 / length), jnp.sqrt(2.0 / length))
    return jnp.cos(phases) * column_scale[None, :]

def damping(level, mode_count):
    mode_ids = jnp.arange(mode_count, dtype=jnp.float32)
    factor = jnp.exp2((3 - level).astype(jnp.float32))
    return 1.0 / (1.0 + (mode_ids * factor / mode_count) ** 2)

def advance(density, lower_rows, upper_rows, courant, diffusion, active):
    vel_cells = density.shape[1]
    velocity = -1.0 + (2.0 * jnp.arange(vel_cells, dtype=jnp.float32) + 1.0) / vel_cells
    upwind = jnp.where(velocity[None, :] > 0, density - lower_rows, upper_rows - density)
    padded_v = jnp.concatenate([density[:, :1], density, density[:, -1:]], axis=1)
    laplace = padded_v[:, 2:] - 2.0 * density + padded_v[:, :-2]
    return density - active * (courant * velocity[None, :] * upwind - diffusion * laplace)

def step_full(density, courant, diffusion, active):
    return advance(density, jnp.roll(density, 1, 0), jnp.roll(density, -1, 0), courant, diffusion, active)

def reference(densities, levels, coeffs):
    basis_x = cosine_basis(jnp.arange(NX, dtype=jnp.float32), MX, NX)
    basis_v = cosine_basis(jnp.arange(NV, dtype=jnp.float32), MV, NV)
    advanced_all = []
    surplus_all = []
    rates = []
    for group in range(GROUPS):
        level_x = levels[group, 0]
        level_v = levels[group, 1]
        courant = 0.3 + level_x.astype(jnp.float32) / 15.0
        diffusion = 0.1 + level_v.astype(jnp.float32) / 30.0
        density = densities[group]
        for step_id in range(PRE):
            active = (step_id < PRE - 3 + level_x).astype(jnp.float32)
            density = step_full(density, courant, diffusion, active)
        reduced = jnp.dot(density, basis_v, precision=HIGHEST_PRECISION)
        projected = jnp.dot(basis_x.T, reduced, precision=HIGHEST_PRECISION)
        own_surplus = damping(level_x, MX)[:, None] * projected * damping(level_v, MV)[None, :]
        advanced_all.append(density)
        surplus_all.append(own_surplus)
        rates.append((courant, diffusion))
    combined = jnp.zeros((MX, MV), jnp.float32)
    for group in range(GROUPS):
        combined = combined + coeffs[group].astype(jnp.float32) * surplus_all[group]
    outputs = []
    for group in range(GROUPS):
        courant, diffusion = rates[group]
        correction = jnp.dot(basis_x, combined - surplus_all[group], precision=HIGHEST_PRECISION)
        density = advanced_all[group] + jnp.dot(correction, basis_v.T, precision=HIGHEST_PRECISION)
        for step_id in range(POST):
            density = step_full(density, courant, diffusion, jnp.float32(1.0))
        outputs.append(density)
    return jnp.stack(outputs)
```

```python
import functools

import jax
import jax.numpy as jnp
import ml_dtypes
import numpy as np
from jax import lax
from jax.experimental import pallas as pl
from jax.experimental.pallas import tpu as pltpu
from jax.sharding import PartitionSpec as P

MX = 2048
MV = 256
PRE = 8
POST = 2
LANES = 128
HALO = 16
AXES = ("comp", "dom")
F32 = jnp.float32
BF16 = jnp.bfloat16


def split_table(table):
    high = table.astype(ml_dtypes.bfloat16)
    low = (table - high.astype(np.float64)).astype(ml_dtypes.bfloat16)
    return high, low


def cosine_table(length, mode_ids, positions):
    scale = np.where(mode_ids == 0, np.sqrt(1.0 / length), np.sqrt(2.0 / length))
    turns = ((2 * positions[:, None] + 1) * mode_ids[None, :]) % (4 * length)
    return np.cos(np.pi * turns / (2.0 * length)) * scale[None, :]


def split(value):
    high = value.astype(BF16)
    return high, (value - high.astype(F32)).astype(BF16)


def dot(a, b, dims=((1,), (0,))):
    return lax.dot_general(a, b, (dims, ((), ())), preferred_element_type=F32)


def rates(levels_ref):
    level_x, level_v = levels_ref[0, 0], levels_ref[0, 1]
    courant = 0.3 + level_x.astype(F32) / 15.0
    diffusion = 0.1 + level_v.astype(F32) / 30.0
    return level_x, courant, diffusion


def fill_coefs(coef, blocks, courant, diffusion, scale, last):
    cells = blocks * LANES
    lane = lax.broadcasted_iota(jnp.int32, (8, LANES), 1)
    for c in range(blocks):
        at = (lane + c * LANES).astype(F32)
        speed = courant * jnp.abs(-1.0 + (2.0 * at + 1.0) / cells)
        own = 1.0 - speed - 2.0 * diffusion
        factor = scale if last else 1.0 / diffusion
        coef[0, c] = own * factor
        coef[1, c] = speed * factor


def step(buf, side, edge, coef, base, stride, unrolls, spread=None):
    blocks = buf.shape[0]
    half = blocks // 2
    lane = lax.broadcasted_iota(jnp.int32, (8, LANES), 1)
    first, final = lane == 0, lane == LANES - 1

    def load(c, r):
        return buf[c, pl.ds(base + r, 8, stride=stride), :]

    def store(c, r, value):
        buf[c, pl.ds(base + r, 8, stride=stride), :] = value

    def right(v):
        return pltpu.roll(v, 1, axis=1)

    def left(v):
        return pltpu.roll(v, LANES - 1, axis=1)

    def combine(r, low, cur, windward, left_edge, right_edge):
        count = len(cur)
        rights = [right(v) for v in cur]
        lefts = [left(v) for v in cur]
        for b in range(count):
            from_left = jnp.where(first, left_edge if b == 0 else rights[b - 1], rights[b])
            from_right = jnp.where(final, right_edge if b == count - 1 else lefts[b + 1], lefts[b])
            around = from_left + from_right
            if spread is not None:
                around = around * spread
            c = low + b
            store(c, r, coef[0, c] * cur[b] + coef[1, c] * windward[b] + around)

    for c in range(half):
        edge[c] = load(c, stride)

    def negative(r, cur, windward):
        side[r] = cur[half - 1]
        combine(r, 0, cur, windward, cur[0], left(load(half, r)))

    def negative_rows(i, cur):
        for u in range(unrolls[0]):
            r = i * unrolls[0] + u
            following = [load(c, r + 1) for c in range(half)]
            negative(r, cur, following)
            cur = following
        return cur

    assert (stride - 1) % unrolls[0] == 0 and stride % unrolls[1] == 0
    cur = lax.fori_loop(0, (stride - 1) // unrolls[0], negative_rows, [load(c, 0) for c in range(half)])
    negative(stride - 1, cur, [edge[c] for c in range(half)])

    def positive_rows(i, before):
        for u in range(unrolls[1]):
            r = i * unrolls[1] + u
            cur = [load(half + b, r) for b in range(half)]
            combine(r, half, cur, before, right(side[r]), cur[half - 1])
            before = cur
        return before

    lax.fori_loop(0, stride // unrolls[1], positive_rows, [load(half + b, -1) for b in range(half)])


def advance_kernel(
    levels, cells, above, below, bv_high, bv_low, advanced, reduced, buf, side, edge, coef, high, low, sems, *, stride
):
    blocks = buf.shape[0]
    rows = cells.shape[0]
    copies = []
    for c in range(blocks):
        lanes = pl.ds(c * LANES, LANES)
        for source, at, size in ((cells, HALO, rows), (above, 0, HALO), (below, HALO + rows, HALO)):
            copies.append(pltpu.make_async_copy(source.at[:, lanes], buf.at[c, pl.ds(at, size), :], sems.at[0]))
    for copy in copies:
        copy.start()
    level_x, courant, diffusion = rates(levels)
    count = jnp.clip(PRE - 3 + level_x, 0, PRE)
    scale = lax.fori_loop(0, count - 1, lambda i, s: s * diffusion, jnp.float32(1.0))
    fill_coefs(coef, blocks, courant, diffusion, None, False)
    for copy in copies:
        copy.wait()
    base = HALO + rows // 2 - 4 * stride
    unrolls = (5, 3)

    def inner(i, carry):
        step(buf, side, edge, coef, base, stride, unrolls)
        return carry

    lax.fori_loop(0, count - 1, inner, 0)
    fill_coefs(coef, blocks, courant, diffusion, scale, True)
    step(buf, side, edge, coef, base, stride, unrolls, scale * diffusion)
    out = pltpu.make_async_copy(buf, advanced, sems.at[1])
    out.start()
    for c in range(blocks):
        lanes = pl.ds(c * LANES, LANES)
        high[:, lanes], low[:, lanes] = split(buf[c, pl.ds(HALO, rows), :])
    total = dot(high[...], bv_high[...]) + dot(high[...], bv_low[...]) + dot(low[...], bv_high[...])
    reduced[...] = total.T
    out.wait()


def reverse_lanes(value):
    lane = lax.broadcasted_iota(jnp.int32, value.shape, 1)
    return jnp.take_along_axis(value, LANES - 1 - lane, axis=1)


def combine_kernel(
    meta, reduced, even_high, even_low, odd_high, odd_low, corrected, halo,
    eh_buf, el_buf, oh_buf, ol_buf, even, odd, sems, *, groups, slabs, modes,
):
    tables = ((even_high, eh_buf), (even_low, el_buf), (odd_high, oh_buf), (odd_low, ol_buf))
    copies = [pltpu.make_async_copy(s, d, sems.at[i]) for i, (s, d) in enumerate(tables)]
    for copy in copies:
        copy.start()
    slab_rows = reduced.shape[2]
    parts = slab_rows // LANES
    for g in range(groups):
        rows = pl.ds(8 * g, 8)
        for d in range(slabs // 2):
            for j in range(parts):
                ahead = reduced[g * slabs + d, :, pl.ds(j * LANES, LANES)]
                mirrored = reverse_lanes(
                    reduced[g * slabs + slabs - 1 - d, :, pl.ds((parts - 1 - j) * LANES, LANES)]
                )
                lanes = pl.ds(d * slab_rows + j * LANES, LANES)
                even[rows, lanes] = ahead + mirrored
                odd[rows, lanes] = ahead - mirrored
    own = lax.axis_index(AXES[0]) * slabs + lax.axis_index(AXES[1])
    half_modes = eh_buf.shape[1]
    size = 8 * groups
    row_mode = own * modes + lax.broadcasted_iota(jnp.int32, (8, half_modes), 0)
    column = lax.broadcasted_iota(jnp.int32, (8, half_modes), 1)
    halves = []
    for parity, (source, high_buf, low_buf) in enumerate(((even, eh_buf, el_buf), (odd, oh_buf, ol_buf))):
        high, low = split(source[...])
        copies[2 * parity].wait()
        both = dot(jnp.concatenate([high, low], axis=0), high_buf[...])
        copies[2 * parity + 1].wait()
        projected = both[:size] + both[size:] + dot(high, low_buf[...])
        mode_x = (2 * column + parity).astype(F32)
        surpluses = []
        combined = jnp.zeros((8, half_modes), F32)
        for g in range(groups):
            factor_x = (1 << (3 - meta[g, 0])).astype(F32)
            factor_v = (1 << (3 - meta[g, 1])).astype(F32)
            damping_x = 1.0 / (1.0 + (mode_x * factor_x / MX) ** 2)
            damping_v = 1.0 / (1.0 + (row_mode.astype(F32) * factor_v / MV) ** 2)
            surplus = damping_x * projected[8 * g : 8 * g + 8] * damping_v
            surpluses.append(surplus)
            combined = combined + meta[g, 2].astype(F32) * surplus
        high, low = split(jnp.concatenate([combined - s for s in surpluses], axis=0))
        both = dot(jnp.concatenate([high, low], axis=0), high_buf[...], ((1,), (1,)))
        halves.append(both[:size] + both[size:] + dot(high, low_buf[...], ((1,), (1,))))
    even[...] = halves[0]
    odd[...] = halves[1]
    for g in range(groups):
        rows = pl.ds(8 * g, 8)
        for d in range(slabs // 2):
            for j in range(parts):
                lanes = pl.ds(d * slab_rows + j * LANES, LANES)
                e, o = even[rows, lanes], odd[rows, lanes]
                corrected[g * slabs + d, :, pl.ds(j * LANES, LANES)] = e + o
                corrected[g * slabs + slabs - 1 - d, :, pl.ds((parts - 1 - j) * LANES, LANES)] = reverse_lanes(e - o)
    lane = lax.broadcasted_iota(jnp.int32, (8, LANES), 1)
    for g in range(groups):
        for d in range(slabs):
            before = corrected[g * slabs + (d - 1) % slabs, :, pl.ds((parts - 1) * LANES, LANES)]
            after = corrected[g * slabs + (d + 1) % slabs, :, pl.ds(0, LANES)]
            halo[g * slabs + d] = jnp.where(
                lane < POST, pltpu.roll(before, POST, axis=1), pltpu.roll(after, POST, axis=1)
            )


def correct_kernel(
    levels, advanced, corrected, halo, bvt_high, bvt_low, result, buf, side, edge, coef, sems, *, stride
):
    blocks = buf.shape[0]
    rows = result.shape[0]
    fetch = pltpu.make_async_copy(advanced, buf, sems.at[0])
    fetch.start()
    _, courant, diffusion = rates(levels)
    fill_coefs(coef, blocks, courant, diffusion, None, False)
    wide = jnp.concatenate([corrected[...], halo[...]], axis=1)
    high, low = split(wide.T[: rows + 8])
    fetch.wait()
    width = 2 * LANES
    for c in range(0, blocks, 2):
        lanes = pl.ds(c * LANES, width)
        right_high, right_low = bvt_high[:, lanes], bvt_low[:, lanes]
        change = dot(high, right_high) + dot(high, right_low) + dot(low, right_high)
        for k in range(2):
            part = change[:, k * LANES : (k + 1) * LANES]
            buf[c + k, pl.ds(HALO, rows), :] += part[:rows]
            buf[c + k, pl.ds(HALO - POST, POST), :] += part[rows : rows + POST]
            buf[c + k, pl.ds(HALO + rows, POST), :] += part[rows + POST : rows + 2 * POST]
    base = HALO + rows // 2 - 4 * stride
    unrolls = (6, 7)
    for _ in range(POST - 1):
        step(buf, side, edge, coef, base, stride, unrolls)
    scale = jnp.float32(1.0)
    for _ in range(POST - 1):
        scale = scale * diffusion
    fill_coefs(coef, blocks, courant, diffusion, scale, True)
    step(buf, side, edge, coef, base, stride, unrolls, scale * diffusion)
    copies = [
        pltpu.make_async_copy(
            buf.at[c, pl.ds(HALO, rows), :], result.at[:, pl.ds(c * LANES, LANES)], sems.at[1]
        )
        for c in range(blocks)
    ]
    for copy in copies:
        copy.start()
    for copy in copies:
        copy.wait()


def body(densities, levels, coeffs):
    density = densities[0]
    rows, cells = density.shape
    groups, slabs = lax.axis_size("comp"), lax.axis_size("dom")
    devices = groups * slabs
    modes = MV // devices
    blocks = cells // LANES
    assert modes * devices == MV and modes <= 8 and slabs % 2 == 0 and blocks % 4 == 0
    half_x, half_modes = rows * slabs // 2, MX // 2

    table = cosine_table(cells, np.arange(MV), np.arange(cells))
    bv_high, bv_low = split_table(table)
    bvt_high, bvt_low = split_table(np.ascontiguousarray(table.T))
    tables_x = []
    for parity in range(2):
        tables_x += split_table(cosine_table(2 * half_x, 2 * np.arange(half_modes) + parity, np.arange(half_x)))

    vmem = pl.BlockSpec(memory_space=pltpu.VMEM)
    smem = pl.BlockSpec(memory_space=pltpu.SMEM)
    hbm = pl.BlockSpec(memory_space=pl.ANY)
    ring = [(i, (i + 1) % slabs) for i in range(slabs)]
    above = lax.ppermute(density[rows - HALO :], "dom", ring)
    below = lax.ppermute(density[:HALO], "dom", [(b, a) for a, b in ring])

    tall = rows + 2 * HALO

    def scratch(stride):
        return [
            pltpu.VMEM((blocks, tall, LANES), F32),
            pltpu.VMEM((stride, 8, LANES), F32),
            pltpu.VMEM((blocks // 2, 8, LANES), F32),
            pltpu.VMEM((2, blocks, 8, LANES), F32),
        ]

    stride = (rows + 2 * (PRE + POST)) // 8 + 1
    advanced, reduced = pl.pallas_call(
        functools.partial(advance_kernel, stride=stride),
        out_shape=(
            jax.ShapeDtypeStruct((blocks, tall, LANES), F32),
            jax.ShapeDtypeStruct((MV, rows), F32),
        ),
        in_specs=[smem, hbm, hbm, hbm, vmem, vmem],
        out_specs=(hbm, vmem),
        scratch_shapes=scratch(stride)
        + [pltpu.VMEM((rows, cells), BF16), pltpu.VMEM((rows, cells), BF16), pltpu.SemaphoreType.DMA((2,))],
        name="advance",
    )(levels, density, above, below, bv_high, bv_low)

    parcels = jnp.pad(reduced.reshape(devices, modes, rows), ((0, 0), (0, 8 - modes), (0, 0)))
    parcels = lax.all_to_all(parcels, AXES, 0, 0, tiled=True)
    note = jnp.concatenate([levels[0], coeffs])
    note = jnp.broadcast_to(jnp.pad(note, (0, LANES - 3)), (groups, 1, LANES))
    meta = lax.all_to_all(note, "comp", 0, 0, tiled=True).reshape(groups, LANES)

    corrected, halo = pl.pallas_call(
        functools.partial(combine_kernel, groups=groups, slabs=slabs, modes=modes),
        out_shape=(
            jax.ShapeDtypeStruct((devices, 8, rows), F32),
            jax.ShapeDtypeStruct((devices, 8, LANES), F32),
        ),
        in_specs=[smem, vmem, hbm, hbm, hbm, hbm],
        out_specs=(vmem, vmem),
        scratch_shapes=[pltpu.VMEM((half_x, half_modes), BF16)] * 4
        + [pltpu.VMEM((8 * groups, half_x), F32)] * 2
        + [pltpu.SemaphoreType.DMA((4,))],
        name="combine",
    )(meta, parcels, *tables_x)

    corrected = lax.all_to_all(corrected, AXES, 0, 0, tiled=True)
    corrected = corrected[:, :modes].reshape(MV, rows)
    ends = halo[:, :modes, : 2 * POST].reshape(devices, 1, modes * 2 * POST)
    ends = lax.all_to_all(ends, AXES, 0, 0, tiled=True).reshape(MV, 2 * POST)
    ends = jnp.pad(ends, ((0, 0), (0, LANES - 2 * POST)))

    stride = (rows + 2 * POST) // 8 + 1
    result = pl.pallas_call(
        functools.partial(correct_kernel, stride=stride),
        out_shape=jax.ShapeDtypeStruct((rows, cells), F32),
        in_specs=[smem, hbm, vmem, vmem, vmem, vmem],
        out_specs=hbm,
        scratch_shapes=scratch(stride) + [pltpu.SemaphoreType.DMA((2,))],
        name="correct",
    )(levels, advanced, corrected, ends, bvt_high, bvt_low)
    return result[None]


def solution(mesh):
    placed = (P("comp", "dom", None), P("comp", None), P("comp"))
    return jax.shard_map(
        body, mesh=mesh, in_specs=placed, out_specs=P("comp", "dom", None), check_vma=False
    )
```

```python
import functools

import jax
import jax.numpy as jnp
import ml_dtypes
import numpy as np
from jax import lax
from jax.experimental import pallas as pl
from jax.experimental.pallas import tpu as pltpu
from jax.sharding import PartitionSpec as P

MX = 2048
MV = 256
PRE = 8
POST = 2
LANES = 128
HALO = 16
PHASES = 4
MARGIN = 8
GUARD = 8
AXES = ("comp", "dom")
F32 = jnp.float32
BF16 = jnp.bfloat16


def split_table(table):
    high = table.astype(ml_dtypes.bfloat16)
    low = (table - high.astype(np.float64)).astype(ml_dtypes.bfloat16)
    return high, low


def cosine_table(length, mode_ids, positions):
    scale = np.where(mode_ids == 0, np.sqrt(1.0 / length), np.sqrt(2.0 / length))
    turns = ((2 * positions[:, None] + 1) * mode_ids[None, :]) % (4 * length)
    return np.cos(np.pi * turns / (2.0 * length)) * scale[None, :]


def split(value):
    high = value.astype(BF16)
    return high, (value - high.astype(F32)).astype(BF16)


def dot(a, b, dims=((1,), (0,))):
    return lax.dot_general(a, b, (dims, ((), ())), preferred_element_type=F32)


def rates(levels_ref):
    level_x, level_v = levels_ref[0, 0], levels_ref[0, 1]
    courant = 0.3 + level_x.astype(F32) / 15.0
    diffusion = 0.1 + level_v.astype(F32) / 30.0
    return level_x, courant, diffusion


def fill_coefs(coef, cells, courant, diffusion):
    size = 128
    inverse = 1.0 / diffusion

    def rows(i, carry):
        at = (i * size + lax.broadcasted_iota(jnp.int32, (size, LANES), 0)).astype(F32)
        speed = courant * jnp.abs(-1.0 + (2.0 * at + 1.0) / cells)
        where = pl.ds(pl.multiple_of(GUARD + i * size, 8), size)
        coef[0, where, :] = (1.0 - speed - 2.0 * diffusion) * inverse
        coef[1, where, :] = speed * inverse
        return carry

    lax.fori_loop(0, cells // size, rows, 0)


def mirror_edges(buf, cells):
    for t in range(PHASES):
        buf[t, pl.ds(GUARD - 1, 1), :] = buf[t, pl.ds(GUARD, 1), :]
        buf[t, pl.ds(GUARD + cells, 1), :] = buf[t, pl.ds(GUARD + cells - 1, 1), :]


def stepped(src, coef, row, size, leftward):
    here = pl.ds(row, size)
    own, windward = coef[0, here, :], coef[1, here, :]
    cur = [src[t, here, :] for t in range(PHASES)]
    if leftward:
        wind = cur[1:] + [pltpu.roll(cur[0], LANES - 1, axis=1)]
    else:
        wind = [pltpu.roll(cur[-1], 1, axis=1)] + cur[:-1]
    return [
        own * cur[t]
        + windward * wind[t]
        + (src[t, pl.ds(row - 1, size), :] + src[t, pl.ds(row + 1, size), :])
        for t in range(PHASES)
    ]


def inner_step(src, dst, coef, cells):
    unroll = 32
    for leftward in (True, False):
        start = GUARD if leftward else GUARD + cells // 2

        def rows(i, carry):
            for k in range(unroll):
                row = pl.multiple_of(start + (i * unroll + k) * 8, 8)
                for t, value in enumerate(stepped(src, coef, row, 8, leftward)):
                    dst[t, pl.ds(row, 8), :] = value
            return carry

        lax.fori_loop(0, cells // 16 // unroll, rows, 0)
    mirror_edges(dst, cells)


def moved_lanes(pieces):
    out = None
    for source, origin, target, count in pieces:
        shift = (target - origin) % LANES
        moved = pltpu.roll(source, shift, axis=1) if shift else source
        if out is None:
            out = moved
        else:
            lane = lax.broadcasted_iota(jnp.int32, moved.shape, 1)
            out = jnp.where((lane >= target) & (lane < target + count), moved, out)
    return out


def overlaps(rows):
    quarter = rows // PHASES
    runs = []
    for j in range(rows // LANES):
        for t in range(PHASES):
            low, high = max(LANES * j, quarter * t), min(LANES * (j + 1), quarter * (t + 1))
            if low < high:
                runs.append((j, t, low - LANES * j, MARGIN + low - quarter * t, high - low))
    return runs


def packed_lane(rows, x):
    return (x % PHASES) * (rows // PHASES) + x // PHASES


def advance_kernel(
    levels, cells, above, below, bvt_high, bvt_low, advanced, reduced,
    natural, first, second, third, coef, high, low, fetches, sems,
):
    rows, width = cells.shape
    planes = width // LANES
    start = PHASES * MARGIN
    fetched = []
    for c in range(planes):
        lanes = pl.ds(c * LANES, LANES)
        copies = [
            pltpu.make_async_copy(source.at[:, lanes], natural.at[c, pl.ds(at, size), :], fetches.at[c])
            for source, at, size in ((cells, start, rows), (above, start - HALO, HALO), (below, start + rows, HALO))
        ]
        for copy in copies:
            copy.start()
        fetched.append(copies)
    level_x, courant, diffusion = rates(levels)
    count = jnp.clip(PRE - 3 + level_x, 0, PRE)
    scale = lax.fori_loop(0, count, lambda i, s: s * diffusion, jnp.float32(1.0))
    fill_coefs(coef, width, courant, diffusion)
    top, tail = start - HALO, start + rows + HALO
    for c in range(planes):
        natural[c, pl.ds(0, top), :] = jnp.zeros((top, LANES), F32)
        natural[c, pl.ds(tail, PHASES * LANES - tail), :] = jnp.zeros((PHASES * LANES - tail, LANES), F32)
        for copy in fetched[c]:
            copy.wait()
        for t in range(PHASES):
            first[t, pl.ds(GUARD + c * LANES, LANES), :] = natural[c, pl.ds(t, LANES, stride=PHASES), :].T
    mirror_edges(first, width)
    inner = count - 1

    def pair(i, carry):
        inner_step(first, second, coef, width)
        inner_step(second, first, coef, width)
        return carry

    lax.fori_loop(0, inner // 2, pair, 0)

    def final(src):
        unroll = 16
        for leftward in (True, False):
            begin = 0 if leftward else width // 2

            def body(i, carry):
                for k in range(unroll):
                    row = pl.multiple_of(begin + (i * unroll + k) * 16, 16)
                    for t, value in enumerate(stepped(src, coef, GUARD + row, 16, leftward)):
                        value = value * scale
                        third[t, pl.ds(row, 16), :] = value
                        lanes = pl.ds(t * LANES, LANES)
                        high[pl.ds(row, 16), lanes], low[pl.ds(row, 16), lanes] = split(value)
                return carry

            lax.fori_loop(0, width // 32 // unroll, body, 0)

    @pl.when(inner % 2 == 1)
    def _():
        inner_step(first, second, coef, width)
        final(second)

    @pl.when(inner % 2 == 0)
    def _():
        final(first)

    out = pltpu.make_async_copy(third, advanced, sems.at[0])
    out.start()
    total = dot(bvt_high[...], high[...]) + dot(bvt_low[...], high[...]) + dot(bvt_high[...], low[...])
    for j in range(rows // LANES):
        pieces = [
            (total[:, t * LANES : (t + 1) * LANES], own, packed, n) for b, t, packed, own, n in overlaps(rows) if b == j
        ]
        reduced[:, pl.ds(j * LANES, LANES)] = moved_lanes(pieces)
    out.wait()


def reverse_lanes(value):
    lane = lax.broadcasted_iota(jnp.int32, value.shape, 1)
    return jnp.take_along_axis(value, LANES - 1 - lane, axis=1)


def combine_kernel(
    meta, reduced, even_high, even_low, odd_high, odd_low, corrected, halo,
    eh_buf, el_buf, oh_buf, ol_buf, even, odd, sems, *, groups, slabs, modes,
):
    tables = ((even_high, eh_buf), (even_low, el_buf), (odd_high, oh_buf), (odd_low, ol_buf))
    copies = [pltpu.make_async_copy(s, d, sems.at[i]) for i, (s, d) in enumerate(tables)]
    for copy in copies:
        copy.start()
    slab_rows = reduced.shape[2]
    parts = slab_rows // LANES
    for g in range(groups):
        rows = pl.ds(8 * g, 8)
        for d in range(slabs // 2):
            for j in range(parts):
                ahead = reduced[g * slabs + d, :, pl.ds(j * LANES, LANES)]
                mirrored = reverse_lanes(
                    reduced[g * slabs + slabs - 1 - d, :, pl.ds((parts - 1 - j) * LANES, LANES)]
                )
                lanes = pl.ds(d * slab_rows + j * LANES, LANES)
                even[rows, lanes] = ahead + mirrored
                odd[rows, lanes] = ahead - mirrored
    own = lax.axis_index(AXES[0]) * slabs + lax.axis_index(AXES[1])
    half_modes = eh_buf.shape[1]
    size = 8 * groups
    row_mode = own * modes + lax.broadcasted_iota(jnp.int32, (8, half_modes), 0)
    column = lax.broadcasted_iota(jnp.int32, (8, half_modes), 1)
    halves = []
    for parity, (source, high_buf, low_buf) in enumerate(((even, eh_buf, el_buf), (odd, oh_buf, ol_buf))):
        high, low = split(source[...])
        copies[2 * parity].wait()
        both = dot(jnp.concatenate([high, low], axis=0), high_buf[...])
        copies[2 * parity + 1].wait()
        projected = both[:size] + both[size:] + dot(high, low_buf[...])
        mode_x = (2 * column + parity).astype(F32)
        surpluses = []
        combined = jnp.zeros((8, half_modes), F32)
        for g in range(groups):
            factor_x = (1 << (3 - meta[g, 0])).astype(F32)
            factor_v = (1 << (3 - meta[g, 1])).astype(F32)
            damping_x = 1.0 / (1.0 + (mode_x * factor_x / MX) ** 2)
            damping_v = 1.0 / (1.0 + (row_mode.astype(F32) * factor_v / MV) ** 2)
            surplus = damping_x * projected[8 * g : 8 * g + 8] * damping_v
            surpluses.append(surplus)
            combined = combined + meta[g, 2].astype(F32) * surplus
        high, low = split(jnp.concatenate([combined - s for s in surpluses], axis=0))
        both = dot(jnp.concatenate([high, low], axis=0), high_buf[...], ((1,), (1,)))
        halves.append(both[:size] + both[size:] + dot(high, low_buf[...], ((1,), (1,))))
    even[...] = halves[0]
    odd[...] = halves[1]
    for g in range(groups):
        rows = pl.ds(8 * g, 8)
        for d in range(slabs // 2):
            for j in range(parts):
                lanes = pl.ds(d * slab_rows + j * LANES, LANES)
                e, o = even[rows, lanes], odd[rows, lanes]
                corrected[g * slabs + d, :, pl.ds(j * LANES, LANES)] = e + o
                corrected[g * slabs + slabs - 1 - d, :, pl.ds((parts - 1 - j) * LANES, LANES)] = reverse_lanes(e - o)
    for g in range(groups):
        for d in range(slabs):
            pieces = []
            for h, x in enumerate(halo_rows(slab_rows)):
                other = (d - 1) % slabs if x < 0 else (d + 1) % slabs
                at = packed_lane(slab_rows, x % slab_rows)
                block = corrected[g * slabs + other, :, pl.ds(at // LANES * LANES, LANES)]
                pieces.append((block, at % LANES, h, 1))
            halo[g * slabs + d] = moved_lanes(pieces)


def halo_rows(rows):
    return [x for x in range(-POST, 0)] + [rows + x for x in range(POST)]


def correct_kernel(
    levels, advanced, corrected, halo, bv_high, bv_low, result, first, second, coef, work, natural, fetches, sems
):
    rows, width = result.shape
    planes = width // LANES
    fetched = [
        pltpu.make_async_copy(advanced.at[t], first.at[t, pl.ds(GUARD, width), :], fetches.at[t]) for t in range(PHASES)
    ]
    for copy in fetched:
        copy.start()
    _, courant, diffusion = rates(levels)
    fill_coefs(coef, width, courant, diffusion)
    scale = jnp.float32(1.0)
    for _ in range(POST):
        scale = scale * diffusion
    wide = []
    for t in range(PHASES):
        pieces = [
            (corrected[:, pl.ds(j * LANES, LANES)], packed, own, n) for j, b, packed, own, n in overlaps(rows) if b == t
        ]
        for h, x in enumerate(halo_rows(rows)):
            if (x + PHASES * MARGIN) % PHASES == t:
                pieces.append((halo[...], h, (x + PHASES * MARGIN) // PHASES, 1))
        wide.append(moved_lanes(pieces))
    high, low = split(jnp.concatenate(wide, axis=1))
    for copy in fetched:
        copy.wait()
    size = 2 * LANES
    for i in range(width // size):
        where = pl.ds(i * size, size)
        left_high, left_low = bv_high[where, :], bv_low[where, :]
        change = dot(left_high, high) + dot(left_high, low) + dot(left_low, high)
        for t in range(PHASES):
            first[t, pl.ds(GUARD + i * size, size), :] += change[:, t * LANES : (t + 1) * LANES]
    mirror_edges(first, width)
    source, other = first, second
    for _ in range(POST - 1):
        inner_step(source, other, coef, width)
        source, other = other, source
    copies = []
    for c in range(planes):
        for k in range(LANES // 8):
            for t, value in enumerate(stepped(source, coef, GUARD + c * LANES + 8 * k, 8, c < planes // 2)):
                work[c % 2, t, pl.ds(8 * k, 8), :] = value * scale
        for t in range(PHASES):
            back = work[c % 2, t].T
            natural[c, pl.ds(t, rows // PHASES, stride=PHASES), :] = back[MARGIN : MARGIN + rows // PHASES]
        copies.append(pltpu.make_async_copy(natural.at[c], result.at[:, pl.ds(c * LANES, LANES)], sems.at[0]))
        copies[-1].start()
    for copy in copies:
        copy.wait()


def body(densities, levels, coeffs):
    density = densities[0]
    rows, cells = density.shape
    groups, slabs = lax.axis_size("comp"), lax.axis_size("dom")
    devices = groups * slabs
    modes = MV // devices
    blocks = cells // LANES
    assert modes * devices == MV and modes <= 8 and slabs % 2 == 0 and blocks % 4 == 0
    half_x, half_modes = rows * slabs // 2, MX // 2

    table = cosine_table(cells, np.arange(MV), np.arange(cells))
    bv_high, bv_low = split_table(table)
    bvt_high, bvt_low = split_table(np.ascontiguousarray(table.T))
    packed = np.arange(rows)
    packed = PHASES * (packed % (rows // PHASES)) + packed // (rows // PHASES)
    positions = (rows * np.arange(slabs // 2)[:, None] + packed[None, :]).reshape(-1)
    tables_x = []
    for parity in range(2):
        tables_x += split_table(cosine_table(2 * half_x, 2 * np.arange(half_modes) + parity, positions))

    vmem = pl.BlockSpec(memory_space=pltpu.VMEM)
    smem = pl.BlockSpec(memory_space=pltpu.SMEM)
    hbm = pl.BlockSpec(memory_space=pl.ANY)
    ring = [(i, (i + 1) % slabs) for i in range(slabs)]
    above = lax.ppermute(density[rows - HALO :], "dom", ring)
    below = lax.ppermute(density[:HALO], "dom", [(b, a) for a, b in ring])

    assert rows % LANES == 0 and rows + HALO <= PHASES * (LANES - MARGIN) and PRE + POST <= HALO
    tall = pltpu.VMEM((PHASES, cells + 2 * GUARD, LANES), F32)
    coefs = pltpu.VMEM((2, cells + 2 * GUARD, LANES), F32)
    flat = pltpu.VMEM((cells, PHASES * LANES), BF16)
    advanced, reduced = pl.pallas_call(
        advance_kernel,
        out_shape=(
            jax.ShapeDtypeStruct((PHASES, cells, LANES), F32),
            jax.ShapeDtypeStruct((MV, rows), F32),
        ),
        in_specs=[smem, hbm, hbm, hbm, vmem, vmem],
        out_specs=(hbm, vmem),
        scratch_shapes=[
            pltpu.VMEM((blocks, PHASES * LANES, LANES), F32),
            tall,
            tall,
            pltpu.VMEM((PHASES, cells, LANES), F32),
            coefs,
            flat,
            flat,
            pltpu.SemaphoreType.DMA((blocks,)),
            pltpu.SemaphoreType.DMA((1,)),
        ],
        name="advance",
    )(levels, density, above, below, bvt_high, bvt_low)

    parcels = jnp.pad(reduced.reshape(devices, modes, rows), ((0, 0), (0, 8 - modes), (0, 0)))
    parcels = lax.all_to_all(parcels, AXES, 0, 0, tiled=True)
    note = jnp.concatenate([levels[0], coeffs])
    note = jnp.broadcast_to(jnp.pad(note, (0, LANES - 3)), (groups, 1, LANES))
    meta = lax.all_to_all(note, "comp", 0, 0, tiled=True).reshape(groups, LANES)

    corrected, halo = pl.pallas_call(
        functools.partial(combine_kernel, groups=groups, slabs=slabs, modes=modes),
        out_shape=(
            jax.ShapeDtypeStruct((devices, 8, rows), F32),
            jax.ShapeDtypeStruct((devices, 8, LANES), F32),
        ),
        in_specs=[smem, vmem, hbm, hbm, hbm, hbm],
        out_specs=(vmem, vmem),
        scratch_shapes=[pltpu.VMEM((half_x, half_modes), BF16)] * 4
        + [pltpu.VMEM((8 * groups, half_x), F32)] * 2
        + [pltpu.SemaphoreType.DMA((4,))],
        name="combine",
    )(meta, parcels, *tables_x)

    corrected = lax.all_to_all(corrected, AXES, 0, 0, tiled=True)
    corrected = corrected[:, :modes].reshape(MV, rows)
    ends = halo[:, :modes, : 2 * POST].reshape(devices, 1, modes * 2 * POST)
    ends = lax.all_to_all(ends, AXES, 0, 0, tiled=True).reshape(MV, 2 * POST)
    ends = jnp.pad(ends, ((0, 0), (0, LANES - 2 * POST)))

    result = pl.pallas_call(
        correct_kernel,
        out_shape=jax.ShapeDtypeStruct((rows, cells), F32),
        in_specs=[smem, hbm, vmem, vmem, vmem, vmem],
        out_specs=hbm,
        scratch_shapes=[
            tall,
            tall,
            coefs,
            pltpu.VMEM((2, PHASES, LANES, LANES), F32),
            pltpu.VMEM((blocks, rows, LANES), F32),
            pltpu.SemaphoreType.DMA((PHASES,)),
            pltpu.SemaphoreType.DMA((1,)),
        ],
        name="correct",
    )(levels, advanced, corrected, ends, bv_high, bv_low)
    return result[None]


def solution(mesh):
    placed = (P("comp", "dom", None), P("comp", None), P("comp"))
    return jax.shard_map(
        body, mesh=mesh, in_specs=placed, out_specs=P("comp", "dom", None), check_vma=False
    )
```

```python
import functools

import jax
import jax.numpy as jnp
import ml_dtypes
import numpy as np
from jax import lax
from jax.experimental import pallas as pl
from jax.experimental.pallas import tpu as pltpu
from jax.sharding import PartitionSpec as P

MX = 2048
MV = 256
PRE = 8
POST = 2
LANES = 128
HALO = 16
PHASES = 4
MARGIN = 8
GUARD = 8
AXES = ("comp", "dom")
F32 = jnp.float32
BF16 = jnp.bfloat16


def split_table(table):
    high = table.astype(ml_dtypes.bfloat16)
    low = (table - high.astype(np.float64)).astype(ml_dtypes.bfloat16)
    return high, low


def cosine_table(length, mode_ids, positions):
    scale = np.where(mode_ids == 0, np.sqrt(1.0 / length), np.sqrt(2.0 / length))
    turns = ((2 * positions[:, None] + 1) * mode_ids[None, :]) % (4 * length)
    return np.cos(np.pi * turns / (2.0 * length)) * scale[None, :]


def split(value):
    high = value.astype(BF16)
    return high, (value - high.astype(F32)).astype(BF16)


def dot(a, b, dims=((1,), (0,))):
    return lax.dot_general(a, b, (dims, ((), ())), preferred_element_type=F32)


def rates(levels_ref):
    level_x, level_v = levels_ref[0, 0], levels_ref[0, 1]
    courant = 0.3 + level_x.astype(F32) / 15.0
    diffusion = 0.1 + level_v.astype(F32) / 30.0
    return level_x, courant, diffusion


def fill_coefs(coef, cells, courant, diffusion):
    size = 128
    inverse = 1.0 / diffusion

    def rows(i, carry):
        at = (i * size + lax.broadcasted_iota(jnp.int32, (size, LANES), 0)).astype(F32)
        speed = courant * jnp.abs(-1.0 + (2.0 * at + 1.0) / cells)
        where = pl.ds(pl.multiple_of(GUARD + i * size, 8), size)
        coef[0, where, :] = (1.0 - speed - 2.0 * diffusion) * inverse
        coef[1, where, :] = speed * inverse
        return carry

    lax.fori_loop(0, cells // size, rows, 0)


def mirror_edges(buf, cells):
    for t in range(PHASES):
        buf[t, pl.ds(GUARD - 1, 1), :] = buf[t, pl.ds(GUARD, 1), :]
        buf[t, pl.ds(GUARD + cells, 1), :] = buf[t, pl.ds(GUARD + cells - 1, 1), :]


def stepped(src, coef, row, size, leftward):
    here = pl.ds(row, size)
    own, windward = coef[0, here, :], coef[1, here, :]
    cur = [src[t, here, :] for t in range(PHASES)]
    if leftward:
        wind = cur[1:] + [pltpu.roll(cur[0], LANES - 1, axis=1)]
    else:
        wind = [pltpu.roll(cur[-1], 1, axis=1)] + cur[:-1]
    return [
        own * cur[t]
        + windward * wind[t]
        + (src[t, pl.ds(row - 1, size), :] + src[t, pl.ds(row + 1, size), :])
        for t in range(PHASES)
    ]


def inner_step(src, dst, coef, cells):
    unroll = 32
    for leftward in (True, False):
        start = GUARD if leftward else GUARD + cells // 2

        def rows(i, carry):
            for k in range(unroll):
                row = pl.multiple_of(start + (i * unroll + k) * 8, 8)
                for t, value in enumerate(stepped(src, coef, row, 8, leftward)):
                    dst[t, pl.ds(row, 8), :] = value
            return carry

        lax.fori_loop(0, cells // 16 // unroll, rows, 0)
    mirror_edges(dst, cells)


def moved_lanes(pieces):
    out = None
    for source, origin, target, count in pieces:
        shift = (target - origin) % LANES
        moved = pltpu.roll(source, shift, axis=1) if shift else source
        if out is None:
            out = moved
        else:
            lane = lax.broadcasted_iota(jnp.int32, moved.shape, 1)
            out = jnp.where((lane >= target) & (lane < target + count), moved, out)
    return out


def overlaps(rows):
    quarter = rows // PHASES
    runs = []
    for j in range(rows // LANES):
        for t in range(PHASES):
            low, high = max(LANES * j, quarter * t), min(LANES * (j + 1), quarter * (t + 1))
            if low < high:
                runs.append((j, t, low - LANES * j, MARGIN + low - quarter * t, high - low))
    return runs


def parcel_rows(rows):
    return 8 * rows // LANES + 1


def packed_lane(rows, x):
    return (x % PHASES) * (rows // PHASES) + x // PHASES


def advance_kernel(
    levels, coeffs, cells, above, below, bvt_high, bvt_low, advanced, parcels,
    natural, first, second, third, coef, high, low, fetches, sems, *, devices,
):
    rows, width = cells.shape
    planes = width // LANES
    start = PHASES * MARGIN
    fetched = []
    for c in range(planes):
        lanes = pl.ds(c * LANES, LANES)
        fetched.append(
            pltpu.make_async_copy(cells.at[:, lanes], natural.at[c, pl.ds(start, rows), :], fetches.at[c])
        )
        fetched[c].start()
    level_x, courant, diffusion = rates(levels)
    count = jnp.clip(PRE - 3 + level_x, 0, PRE)
    scale = lax.fori_loop(0, count, lambda i, s: s * diffusion, jnp.float32(1.0))
    fill_coefs(coef, width, courant, diffusion)
    top, tail = start - HALO, start + rows + HALO
    for c in range(planes):
        natural[c, pl.ds(0, top), :] = jnp.zeros((top, LANES), F32)
        natural[c, pl.ds(tail, PHASES * LANES - tail), :] = jnp.zeros((PHASES * LANES - tail, LANES), F32)
        lanes = pl.ds(c * LANES, LANES)
        natural[c, pl.ds(top, HALO), :] = above[:, lanes]
        natural[c, pl.ds(start + rows, HALO), :] = below[:, lanes]
        fetched[c].wait()
        for t in range(PHASES):
            first[t, pl.ds(GUARD + c * LANES, LANES), :] = natural[c, pl.ds(t, LANES, stride=PHASES), :].T
    mirror_edges(first, width)
    inner = count - 1

    def pair(i, carry):
        inner_step(first, second, coef, width)
        inner_step(second, first, coef, width)
        return carry

    lax.fori_loop(0, inner // 2, pair, 0)

    def final(src):
        unroll = 16
        for leftward in (True, False):
            begin = 0 if leftward else width // 2

            def body(i, carry):
                for k in range(unroll):
                    row = pl.multiple_of(begin + (i * unroll + k) * 16, 16)
                    for t, value in enumerate(stepped(src, coef, GUARD + row, 16, leftward)):
                        value = value * scale
                        third[t, pl.ds(row, 16), :] = value
                        lanes = pl.ds(t * LANES, LANES)
                        high[pl.ds(row, 16), lanes], low[pl.ds(row, 16), lanes] = split(value)
                return carry

            lax.fori_loop(0, width // 32 // unroll, body, 0)

    @pl.when(inner % 2 == 1)
    def _():
        inner_step(first, second, coef, width)
        final(second)

    @pl.when(inner % 2 == 0)
    def _():
        final(first)

    out = pltpu.make_async_copy(third, advanced, sems.at[0])
    out.start()
    total = dot(bvt_high[...], high[...]) + dot(bvt_low[...], high[...]) + dot(bvt_high[...], low[...])
    modes = bvt_high.shape[0] // devices
    lane = lax.broadcasted_iota(jnp.int32, (1, LANES), 1)
    note = jnp.where(lane == 0, (1 << (3 - level_x)).astype(F32) / MX, 0.0)
    note = jnp.where(lane == 1, (1 << (3 - levels[0, 1])).astype(F32) / MV, note)
    note = jnp.where(lane == 2, coeffs[0].astype(F32), note)
    if modes < 8:
        parcels[...] = jnp.zeros_like(parcels)
    for j in range(rows // LANES):
        pieces = [
            (total[:, t * LANES : (t + 1) * LANES], own, packed, n) for b, t, packed, own, n in overlaps(rows) if b == j
        ]
        packed = moved_lanes(pieces)
        for q in range(devices):
            parcels[pl.ds(parcel_rows(rows) * q + 8 * j, modes), :] = packed[modes * q : modes * (q + 1)]
    for q in range(devices):
        parcels[pl.ds(parcel_rows(rows) * (q + 1) - 1, 1), :] = note
    out.wait()


def rotate_sums(terms):
    total = None
    for factor, value in terms:
        if abs(factor) < 1e-12:
            continue
        if abs(factor - 1.0) < 1e-12:
            total = value if total is None else total + value
        elif abs(factor + 1.0) < 1e-12:
            total = -value if total is None else total - value
        else:
            part = value * np.float32(factor)
            total = part if total is None else total + part
    return total


def slab_angle(slabs, d, s):
    return np.cos(np.pi * d * s / slabs), np.sin(np.pi * d * s / slabs)


def slabs_to_residues(cells):
    slabs = len(cells)
    half = slabs // 2
    plus = {d: cells[d] + cells[slabs - d] for d in range(1, half)}
    minus = {d: cells[d] - cells[slabs - d] for d in range(1, half)}
    out = []
    for s in range(slabs + 1):
        same, other = (plus, minus) if s % 2 == 0 else (minus, plus)
        fixed = [(1.0, cells[0])], []
        middle = slab_angle(slabs, half, s)
        real = fixed[0] + [(middle[0], cells[half])] + [(slab_angle(slabs, d, s)[0], same[d]) for d in range(1, half)]
        imag = [(middle[1], cells[half])] + [(slab_angle(slabs, d, s)[1], other[d]) for d in range(1, half)]
        out.append((rotate_sums(real), rotate_sums(imag)))
    return out


def residues_to_slabs(values):
    slabs = len(values) - 1
    out = [None] * slabs
    for d in range(slabs // 2 + 1):
        first, second = [], []
        for s, (real, imag) in enumerate(values):
            cosine, sine = slab_angle(slabs, d, s)
            (first if s % 2 == 0 else second).append((cosine, real))
            if imag is not None:
                (second if s % 2 == 0 else first).append((-sine, imag))
        one, two = rotate_sums(first), rotate_sums(second)
        out[d] = one if two is None else one + two
        if 0 < d < slabs // 2:
            out[slabs - d] = one if two is None else one - two
    return out


def residue_table(rows, slabs, positions):
    used = MX // (2 * slabs)
    count = -(-used // LANES) * LANES
    q = np.arange(count)
    scale = np.where(q < used, np.sqrt(2.0 / (rows * slabs)), 0.0)[None, :]
    blocks = []
    for shift, sign in ((0, -1.0), (1, 1.0)):
        turns = ((2 * positions[:, None] + 1) * (q + shift)[None, :]) % (2 * rows)
        angle = np.pi * turns / rows
        blocks.append(np.concatenate([np.cos(angle) * scale, sign * np.sin(angle) * scale], axis=0))
    return np.concatenate(blocks, axis=1)


def twiddle_table(rows, slabs, positions):
    s = np.arange(slabs + 1)[:, None]
    angle = np.pi * ((2 * positions[None, :] + 1) * s) / (2.0 * rows * slabs)
    return np.stack([np.cos(angle), np.sin(angle)]).astype(np.float32)[:, :, None, :]


def combine_kernel(
    parcels, twiddle, ahead_high, ahead_low, back_high, back_low, corrected, waves, *, groups, slabs, modes
):
    slab_rows = twiddle.shape[3]
    parts = slab_rows // LANES
    each = parcel_rows(slab_rows)
    block = 8 * groups
    for g in range(groups):
        for j in range(parts):
            lanes = pl.ds(j * LANES, LANES)
            cells = [parcels[pl.ds(each * (g * slabs + d) + 8 * j, 8), :] for d in range(slabs)]
            for s, (real, imag) in enumerate(slabs_to_residues(cells)):
                where = pl.ds(s * block + 8 * g, 8)
                cosine, sine = twiddle[0, s, :, lanes], twiddle[1, s, :, lanes]
                if s == 0:
                    turned = real, jnp.zeros_like(real)
                elif imag is None:
                    turned = real * cosine, real * sine
                else:
                    turned = real * cosine - imag * sine, real * sine + imag * cosine
                waves[where, lanes] = turned[0]
                waves[where, pl.ds(slab_rows + j * LANES, LANES)] = turned[1]
    high, low = split(waves[...])
    projected = dot(high, ahead_high[...]) + dot(low, ahead_high[...]) + dot(high, ahead_low[...])
    width = projected.shape[1]
    own = lax.axis_index(AXES[0]) * slabs + lax.axis_index(AXES[1])
    row_mode = (own * modes + lax.broadcasted_iota(jnp.int32, (8, width), 0)).astype(F32)
    column = lax.broadcasted_iota(jnp.int32, (8, width), 1)
    rightward = column >= width // 2
    notes = [parcels[pl.ds(each * (g * slabs + 1) - 1, 1), :] for g in range(groups)]
    factors_x = [jnp.broadcast_to(note[:, 0:1], (8, width)) for note in notes]
    dampings_v = [1.0 / (1.0 + (row_mode * note[:, 1:2]) ** 2) for note in notes]
    weights = [jnp.broadcast_to(note[:, 2:3], (8, width)) for note in notes]
    changes = []
    for s in range(slabs + 1):
        mode_x = jnp.where(
            rightward, 2 * slabs * (column - width // 2) + 2 * slabs - s, 2 * slabs * column + s
        )
        keep = jnp.where(mode_x == 0, 0.5, 1.0)
        if s in (0, slabs):
            keep = jnp.where(rightward, 0.0, keep)
        mode_x = mode_x.astype(F32)
        surpluses = []
        combined = None
        for g in range(groups):
            damping_x = 1.0 / (1.0 + (mode_x * factors_x[g]) ** 2)
            where = s * block + 8 * g
            surplus = damping_x * projected[where : where + 8] * dampings_v[g] * keep
            surpluses.append(surplus)
            part = weights[g] * surplus
            combined = part if combined is None else combined + part
        changes += [combined - surplus for surplus in surpluses]
    high, low = split(jnp.concatenate(changes, axis=0))
    waves[...] = dot(high, back_high[...]) + dot(low, back_high[...]) + dot(high, back_low[...])
    for g in range(groups):
        for j in range(parts):
            lanes = pl.ds(j * LANES, LANES)
            values = []
            for s in range(slabs + 1):
                where = pl.ds(s * block + 8 * g, 8)
                real, imag = waves[where, lanes], waves[where, pl.ds(slab_rows + j * LANES, LANES)]
                cosine, sine = twiddle[0, s, :, lanes], twiddle[1, s, :, lanes]
                if s == 0:
                    values.append((real, None))
                elif s == slabs:
                    values.append((real * cosine + imag * sine, None))
                else:
                    values.append((real * cosine + imag * sine, real * sine - imag * cosine))
            for d, value in enumerate(residues_to_slabs(values)):
                corrected[pl.ds(each * (g * slabs + d) + 8 * j, 8), :] = value
    lane = lax.broadcasted_iota(jnp.int32, (8, LANES), 1)
    for g in range(groups):
        for d in range(slabs):
            pieces = []
            for h, x in enumerate(halo_rows(slab_rows)):
                other = (d - 1) % slabs if x < 0 else (d + 1) % slabs
                at = packed_lane(slab_rows, x % slab_rows)
                source = corrected[pl.ds(each * (g * slabs + other) + at // LANES * 8, 8), :]
                pieces.append((source, at % LANES, h, 1))
            ends = jnp.where(lane < 2 * POST, moved_lanes(pieces), 0.0)
            ends = pltpu.roll(ends, 0, axis=1, stride=2 * POST, stride_axis=0)
            corrected[pl.ds(each * (g * slabs + d + 1) - 1, 1), :] = jnp.sum(ends, axis=0, keepdims=True)


def halo_rows(rows):
    return [x for x in range(-POST, 0)] + [rows + x for x in range(POST)]


def correct_kernel(
    levels, advanced, parcels, bv_high, bv_low, result, first, second, coef, work, natural, corrected, halo,
    fetches, sems, *, devices,
):
    rows, width = result.shape
    planes = width // LANES
    fetched = [
        pltpu.make_async_copy(advanced.at[t], first.at[t, pl.ds(GUARD, width), :], fetches.at[t]) for t in range(PHASES)
    ]
    for copy in fetched:
        copy.start()
    _, courant, diffusion = rates(levels)
    fill_coefs(coef, width, courant, diffusion)
    scale = jnp.float32(1.0)
    for _ in range(POST):
        scale = scale * diffusion
    each, modes = parcel_rows(rows), bv_high.shape[1] // devices
    for q in range(devices):
        where = pl.ds(modes * q, modes)
        for j in range(rows // LANES):
            corrected[where, pl.ds(j * LANES, LANES)] = parcels[pl.ds(each * q + 8 * j, modes), :]
    ends = parcels[pl.ds(each - 1, devices, stride=each), :]
    for m in range(modes):
        shift = (LANES - 2 * POST * m) % LANES
        halo[pl.ds(m, devices, stride=modes), :] = pltpu.roll(ends, shift, axis=1) if shift else ends
    wide = []
    for t in range(PHASES):
        pieces = [
            (corrected[:, pl.ds(j * LANES, LANES)], packed, own, n) for j, b, packed, own, n in overlaps(rows) if b == t
        ]
        for h, x in enumerate(halo_rows(rows)):
            if (x + PHASES * MARGIN) % PHASES == t:
                pieces.append((halo[...], h, (x + PHASES * MARGIN) // PHASES, 1))
        wide.append(moved_lanes(pieces))
    high, low = split(jnp.concatenate(wide, axis=1))
    for copy in fetched:
        copy.wait()
    size = 2 * LANES
    for i in range(width // size):
        where = pl.ds(i * size, size)
        left_high, left_low = bv_high[where, :], bv_low[where, :]
        change = dot(left_high, high) + dot(left_high, low) + dot(left_low, high)
        for t in range(PHASES):
            first[t, pl.ds(GUARD + i * size, size), :] += change[:, t * LANES : (t + 1) * LANES]
    mirror_edges(first, width)
    source, other = first, second
    for _ in range(POST - 1):
        inner_step(source, other, coef, width)
        source, other = other, source
    copies = []
    for c in range(planes):
        for k in range(LANES // 8):
            for t, value in enumerate(stepped(source, coef, GUARD + c * LANES + 8 * k, 8, c < planes // 2)):
                work[c % 2, t, pl.ds(8 * k, 8), :] = value * scale
        for t in range(PHASES):
            back = work[c % 2, t].T
            natural[c, pl.ds(t, rows // PHASES, stride=PHASES), :] = back[MARGIN : MARGIN + rows // PHASES]
        copies.append(pltpu.make_async_copy(natural.at[c], result.at[:, pl.ds(c * LANES, LANES)], sems.at[0]))
        copies[-1].start()
    for copy in copies:
        copy.wait()


def body(densities, levels, coeffs):
    density = densities[0]
    rows, cells = density.shape
    groups, slabs = lax.axis_size("comp"), lax.axis_size("dom")
    devices = groups * slabs
    modes = MV // devices
    blocks = cells // LANES
    assert modes * devices == MV and modes <= 8 and slabs % 2 == 0 and blocks % 4 == 0 and MX % (2 * slabs) == 0

    table = cosine_table(cells, np.arange(MV), np.arange(cells))
    bv_high, bv_low = split_table(table)
    bvt_high, bvt_low = split_table(np.ascontiguousarray(table.T))
    packed = np.arange(rows)
    packed = PHASES * (packed % (rows // PHASES)) + packed // (rows // PHASES)
    ahead = residue_table(rows, slabs, packed)
    tables_x = [twiddle_table(rows, slabs, packed), *split_table(ahead), *split_table(np.ascontiguousarray(ahead.T))]

    vmem = pl.BlockSpec(memory_space=pltpu.VMEM)
    smem = pl.BlockSpec(memory_space=pltpu.SMEM)
    hbm = pl.BlockSpec(memory_space=pl.ANY)
    ring = [(i, (i + 1) % slabs) for i in range(slabs)]
    above = lax.ppermute(density[rows - HALO :], "dom", ring)
    below = lax.ppermute(density[:HALO], "dom", [(b, a) for a, b in ring])

    assert rows % LANES == 0 and rows + HALO <= PHASES * (LANES - MARGIN) and PRE + POST <= HALO
    tall = pltpu.VMEM((PHASES, cells + 2 * GUARD, LANES), F32)
    coefs = pltpu.VMEM((2, cells + 2 * GUARD, LANES), F32)
    flat = pltpu.VMEM((cells, PHASES * LANES), BF16)
    each = parcel_rows(rows)

    def exchange(parcels):
        flat_parcels = parcels.reshape(devices, 1, each * LANES)
        return lax.all_to_all(flat_parcels, AXES, 0, 0, tiled=True).reshape(devices * each, LANES)

    parcels_shape = jax.ShapeDtypeStruct((devices * each, LANES), F32)
    advanced, parcels = pl.pallas_call(
        functools.partial(advance_kernel, devices=devices),
        out_shape=(jax.ShapeDtypeStruct((PHASES, cells, LANES), F32), parcels_shape),
        in_specs=[smem, smem, hbm, vmem, vmem, vmem, vmem],
        out_specs=(hbm, vmem),
        scratch_shapes=[
            pltpu.VMEM((blocks, PHASES * LANES, LANES), F32),
            tall,
            tall,
            pltpu.VMEM((PHASES, cells, LANES), F32),
            coefs,
            flat,
            flat,
            pltpu.SemaphoreType.DMA((blocks,)),
            pltpu.SemaphoreType.DMA((1,)),
        ],
        name="advance",
    )(levels, coeffs, density, above, below, bvt_high, bvt_low)

    parcels = pl.pallas_call(
        functools.partial(combine_kernel, groups=groups, slabs=slabs, modes=modes),
        out_shape=parcels_shape,
        in_specs=[vmem] * 6,
        out_specs=vmem,
        scratch_shapes=[pltpu.VMEM((8 * groups * (slabs + 1), 2 * rows), F32)],
        name="combine",
    )(exchange(parcels), *tables_x)

    result = pl.pallas_call(
        functools.partial(correct_kernel, devices=devices),
        out_shape=jax.ShapeDtypeStruct((rows, cells), F32),
        in_specs=[smem, hbm, vmem, vmem, vmem],
        out_specs=hbm,
        scratch_shapes=[
            tall,
            tall,
            coefs,
            pltpu.VMEM((2, PHASES, LANES, LANES), F32),
            pltpu.VMEM((blocks, rows, LANES), F32),
            pltpu.VMEM((MV, rows), F32),
            pltpu.VMEM((MV, LANES), F32),
            pltpu.SemaphoreType.DMA((PHASES,)),
            pltpu.SemaphoreType.DMA((1,)),
        ],
        name="correct",
    )(levels, advanced, exchange(parcels), bv_high, bv_low)
    return result[None]


def solution(mesh):
    placed = (P("comp", "dom", None), P("comp", None), P("comp"))
    return jax.shard_map(
        body, mesh=mesh, in_specs=placed, out_specs=P("comp", "dom", None), check_vma=False
    )
```

```python
import functools

import jax
import jax.numpy as jnp
import ml_dtypes
import numpy as np
from jax import lax
from jax.experimental import pallas as pl
from jax.experimental.pallas import tpu as pltpu
from jax.sharding import PartitionSpec as P

MX = 2048
MV = 256
PRE = 8
POST = 2
LANES = 128
HALO = 16
PHASES = 4
MARGIN = 8
GUARD = 8
VMEM_LIMIT = 32 * 2**20
AXES = ("comp", "dom")
F32 = jnp.float32
BF16 = jnp.bfloat16


def split_table(table):
    high = table.astype(ml_dtypes.bfloat16)
    low = (table - high.astype(np.float64)).astype(ml_dtypes.bfloat16)
    return high, low


def cosine_table(length, mode_ids, positions):
    scale = np.where(mode_ids == 0, np.sqrt(1.0 / length), np.sqrt(2.0 / length))
    turns = ((2 * positions[:, None] + 1) * mode_ids[None, :]) % (4 * length)
    return np.cos(np.pi * turns / (2.0 * length)) * scale[None, :]


def split(value):
    high = value.astype(BF16)
    return high, (value - high.astype(F32)).astype(BF16)


def dot(a, b, dims=((1,), (0,))):
    return lax.dot_general(a, b, (dims, ((), ())), preferred_element_type=F32)


def rates(levels_ref):
    level_x, level_v = levels_ref[0, 0], levels_ref[0, 1]
    courant = 0.3 + level_x.astype(F32) / 15.0
    diffusion = 0.1 + level_v.astype(F32) / 30.0
    return level_x, courant, diffusion


def fill_coefs(coef, cells, courant, diffusion):
    size = 128
    inverse = 1.0 / diffusion

    def rows(i, carry):
        at = (i * size + lax.broadcasted_iota(jnp.int32, (size, LANES), 0)).astype(F32)
        speed = courant * jnp.abs(-1.0 + (2.0 * at + 1.0) / cells)
        where = pl.ds(pl.multiple_of(GUARD + i * size, 8), size)
        coef[0, where, :] = (1.0 - speed - 2.0 * diffusion) * inverse
        coef[1, where, :] = speed * inverse
        return carry

    lax.fori_loop(0, cells // size, rows, 0)


def mirror_edges(buf, cells):
    for t in range(PHASES):
        buf[t, pl.ds(GUARD - 1, 1), :] = buf[t, pl.ds(GUARD, 1), :]
        buf[t, pl.ds(GUARD + cells, 1), :] = buf[t, pl.ds(GUARD + cells - 1, 1), :]


def stepped(src, coef, row, size, leftward):
    here = pl.ds(row, size)
    own, windward = coef[0, here, :], coef[1, here, :]
    cur = [src[t, here, :] for t in range(PHASES)]
    if leftward:
        wind = cur[1:] + [pltpu.roll(cur[0], LANES - 1, axis=1)]
    else:
        wind = [pltpu.roll(cur[-1], 1, axis=1)] + cur[:-1]
    return [
        own * cur[t]
        + windward * wind[t]
        + (src[t, pl.ds(row - 1, size), :] + src[t, pl.ds(row + 1, size), :])
        for t in range(PHASES)
    ]


def inner_step(src, dst, coef, cells):
    unroll = 32
    for leftward in (True, False):
        start = GUARD if leftward else GUARD + cells // 2

        def rows(i, carry):
            for k in range(unroll):
                row = pl.multiple_of(start + (i * unroll + k) * 8, 8)
                for t, value in enumerate(stepped(src, coef, row, 8, leftward)):
                    dst[t, pl.ds(row, 8), :] = value
            return carry

        lax.fori_loop(0, cells // 16 // unroll, rows, 0)
    mirror_edges(dst, cells)


def moved_lanes(pieces):
    out = None
    for source, origin, target, count in pieces:
        shift = (target - origin) % LANES
        moved = pltpu.roll(source, shift, axis=1) if shift else source
        if out is None:
            out = moved
        else:
            lane = lax.broadcasted_iota(jnp.int32, moved.shape, 1)
            out = jnp.where((lane >= target) & (lane < target + count), moved, out)
    return out


def overlaps(rows):
    quarter = rows // PHASES
    runs = []
    for j in range(rows // LANES):
        for t in range(PHASES):
            low, high = max(LANES * j, quarter * t), min(LANES * (j + 1), quarter * (t + 1))
            if low < high:
                runs.append((j, t, low - LANES * j, MARGIN + low - quarter * t, high - low))
    return runs


def parcel_rows(rows):
    return 8 * rows // LANES + 1


def packed_lane(rows, x):
    return (x % PHASES) * (rows // PHASES) + x // PHASES


def advance_kernel(
    levels, coeffs, cells, above, below, bvt_high_hbm, bvt_low_hbm, advanced, parcels,
    natural, first, second, coef, high, low, bvt_high, bvt_low, fetches, sems, *, devices,
):
    rows, width = cells.shape
    planes = width // LANES
    start = PHASES * MARGIN
    fetched = []
    for c in range(planes):
        lanes = pl.ds(c * LANES, LANES)
        fetched.append(
            pltpu.make_async_copy(cells.at[:, lanes], natural.at[c, pl.ds(start, rows), :], fetches.at[c])
        )
        fetched[c].start()
    tables = [
        pltpu.make_async_copy(bvt_high_hbm, bvt_high, sems.at[0]),
        pltpu.make_async_copy(bvt_low_hbm, bvt_low, sems.at[1]),
    ]
    for copy in tables:
        copy.start()
    level_x, courant, diffusion = rates(levels)
    count = jnp.clip(PRE - 3 + level_x, 0, PRE)
    scale = lax.fori_loop(0, count, lambda i, s: s * diffusion, jnp.float32(1.0))
    fill_coefs(coef, width, courant, diffusion)
    top, tail = start - HALO, start + rows + HALO
    for c in range(planes):
        natural[c, pl.ds(0, top), :] = jnp.zeros((top, LANES), F32)
        natural[c, pl.ds(tail, PHASES * LANES - tail), :] = jnp.zeros((PHASES * LANES - tail, LANES), F32)
        lanes = pl.ds(c * LANES, LANES)
        natural[c, pl.ds(top, HALO), :] = above[:, lanes]
        natural[c, pl.ds(start + rows, HALO), :] = below[:, lanes]
        fetched[c].wait()
        for t in range(PHASES):
            first[t, pl.ds(GUARD + c * LANES, LANES), :] = natural[c, pl.ds(t, LANES, stride=PHASES), :].T
    mirror_edges(first, width)
    inner = count - 1

    def pair(i, carry):
        inner_step(first, second, coef, width)
        inner_step(second, first, coef, width)
        return carry

    lax.fori_loop(0, inner // 2, pair, 0)

    def final(src):
        unroll = 16
        for leftward in (True, False):
            begin = 0 if leftward else width // 2

            def body(i, carry):
                for k in range(unroll):
                    row = pl.multiple_of(begin + (i * unroll + k) * 16, 16)
                    for t, value in enumerate(stepped(src, coef, GUARD + row, 16, leftward)):
                        value = value * scale
                        advanced[t, pl.ds(row, 16), :] = value
                        lanes = pl.ds(t * LANES, LANES)
                        high[pl.ds(row, 16), lanes], low[pl.ds(row, 16), lanes] = split(value)
                return carry

            lax.fori_loop(0, width // 32 // unroll, body, 0)

    @pl.when(inner % 2 == 1)
    def _():
        inner_step(first, second, coef, width)
        final(second)

    @pl.when(inner % 2 == 0)
    def _():
        final(first)

    for copy in tables:
        copy.wait()
    total = dot(bvt_high[...], high[...]) + dot(bvt_low[...], high[...]) + dot(bvt_high[...], low[...])
    modes = bvt_high.shape[0] // devices
    lane = lax.broadcasted_iota(jnp.int32, (1, LANES), 1)
    note = jnp.where(lane == 0, (1 << (3 - level_x)).astype(F32) / MX, 0.0)
    note = jnp.where(lane == 1, (1 << (3 - levels[0, 1])).astype(F32) / MV, note)
    note = jnp.where(lane == 2, coeffs[0].astype(F32), note)
    if modes < 8:
        parcels[...] = jnp.zeros_like(parcels)
    for j in range(rows // LANES):
        pieces = [
            (total[:, t * LANES : (t + 1) * LANES], own, packed, n) for b, t, packed, own, n in overlaps(rows) if b == j
        ]
        packed = moved_lanes(pieces)
        for q in range(devices):
            parcels[pl.ds(parcel_rows(rows) * q + 8 * j, modes), :] = packed[modes * q : modes * (q + 1)]
    for q in range(devices):
        parcels[pl.ds(parcel_rows(rows) * (q + 1) - 1, 1), :] = note


def rotate_sums(terms):
    total = None
    for factor, value in terms:
        if abs(factor) < 1e-12:
            continue
        if abs(factor - 1.0) < 1e-12:
            total = value if total is None else total + value
        elif abs(factor + 1.0) < 1e-12:
            total = -value if total is None else total - value
        else:
            part = value * np.float32(factor)
            total = part if total is None else total + part
    return total


def slab_angle(slabs, d, s):
    return np.cos(np.pi * d * s / slabs), np.sin(np.pi * d * s / slabs)


def slabs_to_residues(cells):
    slabs = len(cells)
    half = slabs // 2
    plus = {d: cells[d] + cells[slabs - d] for d in range(1, half)}
    minus = {d: cells[d] - cells[slabs - d] for d in range(1, half)}
    out = []
    for s in range(slabs + 1):
        same, other = (plus, minus) if s % 2 == 0 else (minus, plus)
        fixed = [(1.0, cells[0])], []
        middle = slab_angle(slabs, half, s)
        real = fixed[0] + [(middle[0], cells[half])] + [(slab_angle(slabs, d, s)[0], same[d]) for d in range(1, half)]
        imag = [(middle[1], cells[half])] + [(slab_angle(slabs, d, s)[1], other[d]) for d in range(1, half)]
        out.append((rotate_sums(real), rotate_sums(imag)))
    return out


def residues_to_slabs(values):
    slabs = len(values) - 1
    out = [None] * slabs
    for d in range(slabs // 2 + 1):
        first, second = [], []
        for s, (real, imag) in enumerate(values):
            cosine, sine = slab_angle(slabs, d, s)
            (first if s % 2 == 0 else second).append((cosine, real))
            if imag is not None:
                (second if s % 2 == 0 else first).append((-sine, imag))
        one, two = rotate_sums(first), rotate_sums(second)
        out[d] = one if two is None else one + two
        if 0 < d < slabs // 2:
            out[slabs - d] = one if two is None else one - two
    return out


def residue_table(rows, slabs, positions):
    used = MX // (2 * slabs)
    count = -(-used // LANES) * LANES
    q = np.arange(count)
    scale = np.where(q < used, np.sqrt(2.0 / (rows * slabs)), 0.0)[None, :]
    blocks = []
    for shift, sign in ((0, -1.0), (1, 1.0)):
        turns = ((2 * positions[:, None] + 1) * (q + shift)[None, :]) % (2 * rows)
        angle = np.pi * turns / rows
        blocks.append(np.concatenate([np.cos(angle) * scale, sign * np.sin(angle) * scale], axis=0))
    return np.concatenate(blocks, axis=1)


def twiddle_table(rows, slabs, positions):
    s = np.arange(slabs + 1)[:, None]
    angle = np.pi * ((2 * positions[None, :] + 1) * s) / (2.0 * rows * slabs)
    return np.stack([np.cos(angle), np.sin(angle)]).astype(np.float32)[:, :, None, :]


def combine_kernel(
    parcels, twiddle, ahead_high, ahead_low, back_high, back_low, corrected, waves, *, groups, slabs, modes
):
    slab_rows = twiddle.shape[3]
    parts = slab_rows // LANES
    each = parcel_rows(slab_rows)
    block = 8 * groups
    for g in range(groups):
        for j in range(parts):
            lanes = pl.ds(j * LANES, LANES)
            cells = [parcels[pl.ds(each * (g * slabs + d) + 8 * j, 8), :] for d in range(slabs)]
            for s, (real, imag) in enumerate(slabs_to_residues(cells)):
                where = pl.ds(s * block + 8 * g, 8)
                cosine, sine = twiddle[0, s, :, lanes], twiddle[1, s, :, lanes]
                if s == 0:
                    turned = real, jnp.zeros_like(real)
                elif imag is None:
                    turned = real * cosine, real * sine
                else:
                    turned = real * cosine - imag * sine, real * sine + imag * cosine
                waves[where, lanes] = turned[0]
                waves[where, pl.ds(slab_rows + j * LANES, LANES)] = turned[1]
    high, low = split(waves[...])
    projected = dot(high, ahead_high[...]) + dot(low, ahead_high[...]) + dot(high, ahead_low[...])
    width = projected.shape[1]
    own = lax.axis_index(AXES[0]) * slabs + lax.axis_index(AXES[1])
    row_mode = (own * modes + lax.broadcasted_iota(jnp.int32, (8, width), 0)).astype(F32)
    column = lax.broadcasted_iota(jnp.int32, (8, width), 1)
    rightward = column >= width // 2
    notes = [parcels[pl.ds(each * (g * slabs + 1) - 1, 1), :] for g in range(groups)]
    factors_x = [jnp.broadcast_to(note[:, 0:1], (8, width)) for note in notes]
    dampings_v = [1.0 / (1.0 + (row_mode * note[:, 1:2]) ** 2) for note in notes]
    weights = [jnp.broadcast_to(note[:, 2:3], (8, width)) for note in notes]
    changes = []
    for s in range(slabs + 1):
        mode_x = jnp.where(
            rightward, 2 * slabs * (column - width // 2) + 2 * slabs - s, 2 * slabs * column + s
        )
        keep = jnp.where(mode_x == 0, 0.5, 1.0)
        if s in (0, slabs):
            keep = jnp.where(rightward, 0.0, keep)
        mode_x = mode_x.astype(F32)
        surpluses = []
        combined = None
        for g in range(groups):
            damping_x = 1.0 / (1.0 + (mode_x * factors_x[g]) ** 2)
            where = s * block + 8 * g
            surplus = damping_x * projected[where : where + 8] * dampings_v[g] * keep
            surpluses.append(surplus)
            part = weights[g] * surplus
            combined = part if combined is None else combined + part
        changes += [combined - surplus for surplus in surpluses]
    high, low = split(jnp.concatenate(changes, axis=0))
    waves[...] = dot(high, back_high[...]) + dot(low, back_high[...]) + dot(high, back_low[...])
    for g in range(groups):
        for j in range(parts):
            lanes = pl.ds(j * LANES, LANES)
            values = []
            for s in range(slabs + 1):
                where = pl.ds(s * block + 8 * g, 8)
                real, imag = waves[where, lanes], waves[where, pl.ds(slab_rows + j * LANES, LANES)]
                cosine, sine = twiddle[0, s, :, lanes], twiddle[1, s, :, lanes]
                if s == 0:
                    values.append((real, None))
                elif s == slabs:
                    values.append((real * cosine + imag * sine, None))
                else:
                    values.append((real * cosine + imag * sine, real * sine - imag * cosine))
            for d, value in enumerate(residues_to_slabs(values)):
                corrected[pl.ds(each * (g * slabs + d) + 8 * j, 8), :] = value
    lane = lax.broadcasted_iota(jnp.int32, (8, LANES), 1)
    for g in range(groups):
        for d in range(slabs):
            pieces = []
            for h, x in enumerate(halo_rows(slab_rows)):
                other = (d - 1) % slabs if x < 0 else (d + 1) % slabs
                at = packed_lane(slab_rows, x % slab_rows)
                source = corrected[pl.ds(each * (g * slabs + other) + at // LANES * 8, 8), :]
                pieces.append((source, at % LANES, h, 1))
            ends = jnp.where(lane < 2 * POST, moved_lanes(pieces), 0.0)
            ends = pltpu.roll(ends, 0, axis=1, stride=2 * POST, stride_axis=0)
            corrected[pl.ds(each * (g * slabs + d + 1) - 1, 1), :] = jnp.sum(ends, axis=0, keepdims=True)


def halo_rows(rows):
    return [x for x in range(-POST, 0)] + [rows + x for x in range(POST)]


def correct_kernel(
    levels, advanced, parcels, bv_high, bv_low, result, first, second, coef, work, natural, corrected, halo,
    sems, *, devices,
):
    rows, width = result.shape
    planes = width // LANES
    _, courant, diffusion = rates(levels)
    fill_coefs(coef, width, courant, diffusion)
    scale = jnp.float32(1.0)
    for _ in range(POST):
        scale = scale * diffusion
    each, modes = parcel_rows(rows), bv_high.shape[1] // devices
    for q in range(devices):
        where = pl.ds(modes * q, modes)
        for j in range(rows // LANES):
            corrected[where, pl.ds(j * LANES, LANES)] = parcels[pl.ds(each * q + 8 * j, modes), :]
    ends = parcels[pl.ds(each - 1, devices, stride=each), :]
    for m in range(modes):
        shift = (LANES - 2 * POST * m) % LANES
        halo[pl.ds(m, devices, stride=modes), :] = pltpu.roll(ends, shift, axis=1) if shift else ends
    wide = []
    for t in range(PHASES):
        pieces = [
            (corrected[:, pl.ds(j * LANES, LANES)], packed, own, n) for j, b, packed, own, n in overlaps(rows) if b == t
        ]
        for h, x in enumerate(halo_rows(rows)):
            if (x + PHASES * MARGIN) % PHASES == t:
                pieces.append((halo[...], h, (x + PHASES * MARGIN) // PHASES, 1))
        wide.append(moved_lanes(pieces))
    high, low = split(jnp.concatenate(wide, axis=1))
    size = 2 * LANES
    for i in range(width // size):
        where = pl.ds(i * size, size)
        left_high, left_low = bv_high[where, :], bv_low[where, :]
        change = dot(left_high, high) + dot(left_high, low) + dot(left_low, high)
        for t in range(PHASES):
            first[t, pl.ds(GUARD + i * size, size), :] = advanced[t, where, :] + change[:, t * LANES : (t + 1) * LANES]
    mirror_edges(first, width)
    source, other = first, second
    for _ in range(POST - 1):
        inner_step(source, other, coef, width)
        source, other = other, source
    copies = []
    for c in range(planes):
        for k in range(LANES // 8):
            for t, value in enumerate(stepped(source, coef, GUARD + c * LANES + 8 * k, 8, c < planes // 2)):
                work[c % 2, t, pl.ds(8 * k, 8), :] = value * scale
        for t in range(PHASES):
            back = work[c % 2, t].T
            natural[c, pl.ds(t, rows // PHASES, stride=PHASES), :] = back[MARGIN : MARGIN + rows // PHASES]
        copies.append(pltpu.make_async_copy(natural.at[c], result.at[:, pl.ds(c * LANES, LANES)], sems.at[0]))
        copies[-1].start()
    for copy in copies:
        copy.wait()


def in_vmem(value):
    return pltpu.with_memory_space_constraint(value, pltpu.VMEM)


def in_hbm(value):
    return pltpu.with_memory_space_constraint(value, pltpu.HBM)


def body(densities, levels, coeffs):
    density = densities[0]
    rows, cells = density.shape
    groups, slabs = lax.axis_size("comp"), lax.axis_size("dom")
    devices = groups * slabs
    modes = MV // devices
    blocks = cells // LANES
    assert modes * devices == MV and modes <= 8 and slabs % 2 == 0 and blocks % 4 == 0 and MX % (2 * slabs) == 0

    table = cosine_table(cells, np.arange(MV), np.arange(cells))
    bv_high, bv_low = split_table(table)
    bvt_high, bvt_low = split_table(np.ascontiguousarray(table.T))
    packed = np.arange(rows)
    packed = PHASES * (packed % (rows // PHASES)) + packed // (rows // PHASES)
    ahead = residue_table(rows, slabs, packed)
    tables_x = [twiddle_table(rows, slabs, packed), *split_table(ahead), *split_table(np.ascontiguousarray(ahead.T))]

    vmem = pl.BlockSpec(memory_space=pltpu.VMEM)
    smem = pl.BlockSpec(memory_space=pltpu.SMEM)
    hbm = pl.BlockSpec(memory_space=pl.ANY)
    ring = [(i, (i + 1) % slabs) for i in range(slabs)]
    above = in_vmem(lax.ppermute(density[rows - HALO :], "dom", ring))
    below = in_vmem(lax.ppermute(density[:HALO], "dom", [(b, a) for a, b in ring]))

    assert rows % LANES == 0 and rows + HALO <= PHASES * (LANES - MARGIN) and PRE + POST <= HALO
    tall = pltpu.VMEM((PHASES, cells + 2 * GUARD, LANES), F32)
    coefs = pltpu.VMEM((2, cells + 2 * GUARD, LANES), F32)
    flat = pltpu.VMEM((cells, PHASES * LANES), BF16)
    each = parcel_rows(rows)

    def exchange(parcels):
        flat_parcels = parcels.reshape(devices, 1, each * LANES)
        return in_vmem(lax.all_to_all(flat_parcels, AXES, 0, 0, tiled=True).reshape(devices * each, LANES))

    parcels_shape = pltpu.VMEM((devices * each, LANES), F32)
    advanced, parcels = pl.pallas_call(
        functools.partial(advance_kernel, devices=devices),
        out_shape=(pltpu.VMEM((PHASES, cells, LANES), F32), parcels_shape),
        in_specs=[smem, smem, hbm, vmem, vmem, hbm, hbm],
        out_specs=(vmem, vmem),
        scratch_shapes=[
            pltpu.VMEM((blocks, PHASES * LANES, LANES), F32),
            tall,
            tall,
            coefs,
            flat,
            flat,
            pltpu.VMEM((MV, cells), BF16),
            pltpu.VMEM((MV, cells), BF16),
            pltpu.SemaphoreType.DMA((blocks,)),
            pltpu.SemaphoreType.DMA((2,)),
        ],
        compiler_params=pltpu.CompilerParams(vmem_limit_bytes=VMEM_LIMIT),
        name="advance",
    )(in_hbm(levels), coeffs, in_hbm(density), above, below, in_hbm(bvt_high), in_hbm(bvt_low))

    parcels = pl.pallas_call(
        functools.partial(combine_kernel, groups=groups, slabs=slabs, modes=modes),
        out_shape=parcels_shape,
        in_specs=[vmem] * 6,
        out_specs=vmem,
        scratch_shapes=[pltpu.VMEM((8 * groups * (slabs + 1), 2 * rows), F32)],
        compiler_params=pltpu.CompilerParams(vmem_limit_bytes=VMEM_LIMIT),
        name="combine",
    )(exchange(parcels), *map(in_vmem, tables_x))

    result = pl.pallas_call(
        functools.partial(correct_kernel, devices=devices),
        out_shape=jax.ShapeDtypeStruct((rows, cells), F32),
        in_specs=[smem, vmem, vmem, vmem, vmem],
        out_specs=hbm,
        scratch_shapes=[
            tall,
            tall,
            coefs,
            pltpu.VMEM((2, PHASES, LANES, LANES), F32),
            pltpu.VMEM((blocks, rows, LANES), F32),
            pltpu.VMEM((MV, rows), F32),
            pltpu.VMEM((MV, LANES), F32),
            pltpu.SemaphoreType.DMA((1,)),
        ],
        compiler_params=pltpu.CompilerParams(vmem_limit_bytes=VMEM_LIMIT),
        name="correct",
    )(in_hbm(levels), advanced, exchange(parcels), in_vmem(bv_high), in_vmem(bv_low))
    return result[None]


def solution(mesh):
    placed = (P("comp", "dom", None), P("comp", None), P("comp"))
    return jax.shard_map(
        body, mesh=mesh, in_specs=placed, out_specs=P("comp", "dom", None), check_vma=False
    )
```

```python
import functools

import jax
import jax.numpy as jnp
import ml_dtypes
import numpy as np
from jax import lax
from jax.experimental import pallas as pl
from jax.experimental.pallas import tpu as pltpu
from jax.sharding import PartitionSpec as P

MX = 2048
MV = 256
PRE = 8
POST = 2
LANES = 128
HALO = 16
PHASES = 4
MARGIN = 8
GUARD = 8
VMEM_LIMIT = 32 * 2**20
AXES = ("comp", "dom")
F32 = jnp.float32
BF16 = jnp.bfloat16


def split_table(table):
    high = table.astype(ml_dtypes.bfloat16)
    low = (table - high.astype(np.float64)).astype(ml_dtypes.bfloat16)
    return high, low


def cosine_table(length, mode_ids, positions):
    scale = np.where(mode_ids == 0, np.sqrt(1.0 / length), np.sqrt(2.0 / length))
    turns = ((2 * positions[:, None] + 1) * mode_ids[None, :]) % (4 * length)
    return np.cos(np.pi * turns / (2.0 * length)) * scale[None, :]


def split(value):
    high = value.astype(BF16)
    return high, (value - high.astype(F32)).astype(BF16)


def dot(a, b, dims=((1,), (0,))):
    return lax.dot_general(a, b, (dims, ((), ())), preferred_element_type=F32)


def rates(levels_ref):
    level_x, level_v = levels_ref[0, 0], levels_ref[0, 1]
    courant = 0.3 + level_x.astype(F32) / 15.0
    diffusion = 0.1 + level_v.astype(F32) / 30.0
    return level_x, courant, diffusion


def fill_coefs(coef, cells, courant, diffusion):
    size = 128
    inverse = 1.0 / diffusion

    def rows(i, carry):
        at = (i * size + lax.broadcasted_iota(jnp.int32, (size, LANES), 0)).astype(F32)
        speed = courant * jnp.abs(-1.0 + (2.0 * at + 1.0) / cells)
        where = pl.ds(pl.multiple_of(GUARD + i * size, 8), size)
        coef[0, where, :] = (1.0 - speed - 2.0 * diffusion) * inverse
        coef[1, where, :] = speed * inverse
        return carry

    lax.fori_loop(0, cells // size, rows, 0)


def mirror_edges(buf, cells):
    for t in range(PHASES):
        buf[t, pl.ds(GUARD - 1, 1), :] = buf[t, pl.ds(GUARD, 1), :]
        buf[t, pl.ds(GUARD + cells, 1), :] = buf[t, pl.ds(GUARD + cells - 1, 1), :]


def stepped(src, coef, row, size, leftward):
    here = pl.ds(row, size)
    own, windward = coef[0, here, :], coef[1, here, :]
    cur = [src[t, here, :] for t in range(PHASES)]
    if leftward:
        wind = cur[1:] + [pltpu.roll(cur[0], LANES - 1, axis=1)]
    else:
        wind = [pltpu.roll(cur[-1], 1, axis=1)] + cur[:-1]
    return [
        own * cur[t]
        + windward * wind[t]
        + (src[t, pl.ds(row - 1, size), :] + src[t, pl.ds(row + 1, size), :])
        for t in range(PHASES)
    ]


def inner_step(src, dst, coef, cells):
    unroll = 32
    for leftward in (True, False):
        start = GUARD if leftward else GUARD + cells // 2

        def rows(i, carry):
            for k in range(unroll):
                row = pl.multiple_of(start + (i * unroll + k) * 8, 8)
                for t, value in enumerate(stepped(src, coef, row, 8, leftward)):
                    dst[t, pl.ds(row, 8), :] = value
            return carry

        lax.fori_loop(0, cells // 16 // unroll, rows, 0)
    mirror_edges(dst, cells)


def moved_lanes(pieces):
    out = None
    for source, origin, target, count in pieces:
        shift = (target - origin) % LANES
        moved = pltpu.roll(source, shift, axis=1) if shift else source
        if out is None:
            out = moved
        else:
            lane = lax.broadcasted_iota(jnp.int32, moved.shape, 1)
            out = jnp.where((lane >= target) & (lane < target + count), moved, out)
    return out


def overlaps(rows):
    quarter = rows // PHASES
    runs = []
    for j in range(rows // LANES):
        for t in range(PHASES):
            low, high = max(LANES * j, quarter * t), min(LANES * (j + 1), quarter * (t + 1))
            if low < high:
                runs.append((j, t, low - LANES * j, MARGIN + low - quarter * t, high - low))
    return runs


def parcel_rows(rows):
    return 8 * rows // LANES + 1


def packed_lane(rows, x):
    return (x % PHASES) * (rows // PHASES) + x // PHASES


def turn_kernel(levels, cells, turned, coef, natural, fetches):
    rows, width = cells.shape
    start = PHASES * MARGIN
    tail = start + rows
    copies = []
    for c in range(width // LANES):
        lanes = pl.ds(c * LANES, LANES)
        copies.append(
            pltpu.make_async_copy(cells.at[:, lanes], natural.at[c, pl.ds(start, rows), :], fetches.at[c])
        )
        copies[c].start()
    _, courant, diffusion = rates(levels)
    fill_coefs(coef, width, courant, diffusion)
    for c, copy in enumerate(copies):
        natural[c, pl.ds(0, start), :] = jnp.zeros((start, LANES), F32)
        natural[c, pl.ds(tail, PHASES * LANES - tail), :] = jnp.zeros((PHASES * LANES - tail, LANES), F32)
        copy.wait()
        for t in range(PHASES):
            turned[t, pl.ds(c * LANES, LANES), :] = natural[c, pl.ds(t, LANES, stride=PHASES), :].T


def advance_kernel(
    levels, coeffs, turned, coef, above, below, bvt_high_hbm, bvt_low_hbm, advanced, parcels,
    first, second, halos, strips, high, low, bvt_high, bvt_low, sems, *, devices, rows,
):
    width = turned.shape[1]
    planes = width // LANES
    tables = [
        pltpu.make_async_copy(bvt_high_hbm, bvt_high, sems.at[0]),
        pltpu.make_async_copy(bvt_low_hbm, bvt_low, sems.at[1]),
    ]
    for copy in tables:
        copy.start()
    level_x, _, diffusion = rates(levels)
    count = jnp.clip(PRE - 3 + level_x, 0, PRE)
    scale = lax.fori_loop(0, count, lambda i, s: s * diffusion, jnp.float32(1.0))
    run = HALO // PHASES
    sides = ((MARGIN - run, 0), (MARGIN + rows // PHASES, HALO))
    shift = 2 * run
    lane = lax.broadcasted_iota(jnp.int32, (LANES, LANES), 1)
    is_halo = jnp.zeros((LANES, LANES), jnp.bool_)
    for low_lane, _ in sides:
        is_halo = is_halo | ((lane >= low_lane) & (lane < low_lane + run))

    def insert(target):
        for c in range(planes):
            lanes = pl.ds(c * LANES, LANES)
            halos[c, pl.ds(0, HALO), :] = above[:, lanes]
            halos[c, pl.ds(HALO, HALO), :] = below[:, lanes]
            for t in range(PHASES):
                for low_lane, row in sides:
                    at = (low_lane + shift * t) % LANES
                    strips[c, pl.ds(at, run), :] = halos[c, pl.ds(row + t, run, stride=PHASES), :]
            strip = strips[c].T
            where = pl.ds(c * LANES, LANES)
            for t in range(PHASES):
                moved = pltpu.roll(strip, LANES - shift * t, axis=1) if t else strip
                target[t, pl.ds(GUARD + c * LANES, LANES), :] = jnp.where(is_halo, moved, turned[t, where, :])
        mirror_edges(target, width)

    inner = count - 1

    @pl.when(inner % 2 == 0)
    def _():
        insert(first)

    @pl.when(inner % 2 == 1)
    def _():
        insert(second)
        inner_step(second, first, coef, width)

    def pair(i, carry):
        inner_step(first, second, coef, width)
        inner_step(second, first, coef, width)
        return carry

    lax.fori_loop(0, inner // 2, pair, 0)
    for copy in tables:
        copy.wait()
    size = 2 * LANES
    total = None
    for i in range(width // size + 1):
        if i < width // size:
            for k in range(size // 16):
                row = i * size + k * 16
                for t, value in enumerate(stepped(first, coef, GUARD + row, 16, row < width // 2)):
                    value = value * scale
                    advanced[t, pl.ds(row, 16), :] = value
                    lanes = pl.ds(t * LANES, LANES)
                    high[pl.ds(row, 16), lanes], low[pl.ds(row, 16), lanes] = split(value)
        if i > 0:
            where = pl.ds((i - 1) * size, size)
            left_high, left_low = bvt_high[:, where], bvt_low[:, where]
            right_high, right_low = high[where, :], low[where, :]
            part = dot(left_high, right_high) + dot(left_low, right_high) + dot(left_high, right_low)
            total = part if total is None else total + part
    modes = bvt_high.shape[0] // devices
    lane = lax.broadcasted_iota(jnp.int32, (1, LANES), 1)
    note = jnp.where(lane == 0, (1 << (3 - level_x)).astype(F32) / MX, 0.0)
    note = jnp.where(lane == 1, (1 << (3 - levels[0, 1])).astype(F32) / MV, note)
    note = jnp.where(lane == 2, coeffs[0].astype(F32), note)
    if modes < 8:
        parcels[...] = jnp.zeros_like(parcels)
    for j in range(rows // LANES):
        pieces = [
            (total[:, t * LANES : (t + 1) * LANES], own, packed, n) for b, t, packed, own, n in overlaps(rows) if b == j
        ]
        packed = moved_lanes(pieces)
        for q in range(devices):
            parcels[pl.ds(parcel_rows(rows) * q + 8 * j, modes), :] = packed[modes * q : modes * (q + 1)]
    for q in range(devices):
        parcels[pl.ds(parcel_rows(rows) * (q + 1) - 1, 1), :] = note


def rotate_sums(terms):
    total = None
    for factor, value in terms:
        if abs(factor) < 1e-12:
            continue
        if abs(factor - 1.0) < 1e-12:
            total = value if total is None else total + value
        elif abs(factor + 1.0) < 1e-12:
            total = -value if total is None else total - value
        else:
            part = value * np.float32(factor)
            total = part if total is None else total + part
    return total


def slab_angle(slabs, d, s):
    return np.cos(np.pi * d * s / slabs), np.sin(np.pi * d * s / slabs)


def slabs_to_residues(cells):
    slabs = len(cells)
    half = slabs // 2
    plus = {d: cells[d] + cells[slabs - d] for d in range(1, half)}
    minus = {d: cells[d] - cells[slabs - d] for d in range(1, half)}
    out = []
    for s in range(slabs + 1):
        same, other = (plus, minus) if s % 2 == 0 else (minus, plus)
        fixed = [(1.0, cells[0])], []
        middle = slab_angle(slabs, half, s)
        real = fixed[0] + [(middle[0], cells[half])] + [(slab_angle(slabs, d, s)[0], same[d]) for d in range(1, half)]
        imag = [(middle[1], cells[half])] + [(slab_angle(slabs, d, s)[1], other[d]) for d in range(1, half)]
        out.append((rotate_sums(real), rotate_sums(imag)))
    return out


def residues_to_slabs(values):
    slabs = len(values) - 1
    out = [None] * slabs
    for d in range(slabs // 2 + 1):
        first, second = [], []
        for s, (real, imag) in enumerate(values):
            cosine, sine = slab_angle(slabs, d, s)
            (first if s % 2 == 0 else second).append((cosine, real))
            if imag is not None:
                (second if s % 2 == 0 else first).append((-sine, imag))
        one, two = rotate_sums(first), rotate_sums(second)
        out[d] = one if two is None else one + two
        if 0 < d < slabs // 2:
            out[slabs - d] = one if two is None else one - two
    return out


def residue_table(rows, slabs, positions):
    used = MX // (2 * slabs)
    count = -(-used // LANES) * LANES
    q = np.arange(count)
    scale = np.where(q < used, np.sqrt(2.0 / (rows * slabs)), 0.0)[None, :]
    blocks = []
    for shift, sign in ((0, -1.0), (1, 1.0)):
        turns = ((2 * positions[:, None] + 1) * (q + shift)[None, :]) % (2 * rows)
        angle = np.pi * turns / rows
        blocks.append(np.concatenate([np.cos(angle) * scale, sign * np.sin(angle) * scale], axis=0))
    return np.concatenate(blocks, axis=1)


def twiddle_table(rows, slabs, positions):
    s = np.arange(slabs + 1)[:, None]
    angle = np.pi * ((2 * positions[None, :] + 1) * s) / (2.0 * rows * slabs)
    return np.stack([np.cos(angle), np.sin(angle)]).astype(np.float32)[:, :, None, :]


def combine_kernel(
    parcels, twiddle, ahead_high, ahead_low, back_high, back_low, corrected, waves, *, groups, slabs, modes
):
    slab_rows = twiddle.shape[3]
    parts = slab_rows // LANES
    each = parcel_rows(slab_rows)
    block = 8 * groups
    for g in range(groups):
        for j in range(parts):
            lanes = pl.ds(j * LANES, LANES)
            cells = [parcels[pl.ds(each * (g * slabs + d) + 8 * j, 8), :] for d in range(slabs)]
            for s, (real, imag) in enumerate(slabs_to_residues(cells)):
                where = pl.ds(s * block + 8 * g, 8)
                cosine, sine = twiddle[0, s, :, lanes], twiddle[1, s, :, lanes]
                if s == 0:
                    turned = real, jnp.zeros_like(real)
                elif imag is None:
                    turned = real * cosine, real * sine
                else:
                    turned = real * cosine - imag * sine, real * sine + imag * cosine
                waves[where, lanes] = turned[0]
                waves[where, pl.ds(slab_rows + j * LANES, LANES)] = turned[1]
    high, low = split(waves[...])
    projected = dot(high, ahead_high[...]) + dot(low, ahead_high[...]) + dot(high, ahead_low[...])
    width = projected.shape[1]
    own = lax.axis_index(AXES[0]) * slabs + lax.axis_index(AXES[1])
    row_mode = (own * modes + lax.broadcasted_iota(jnp.int32, (8, width), 0)).astype(F32)
    column = lax.broadcasted_iota(jnp.int32, (8, width), 1)
    rightward = column >= width // 2
    notes = [parcels[pl.ds(each * (g * slabs + 1) - 1, 1), :] for g in range(groups)]
    factors_x = [jnp.broadcast_to(note[:, 0:1], (8, width)) for note in notes]
    dampings_v = [1.0 / (1.0 + (row_mode * note[:, 1:2]) ** 2) for note in notes]
    weights = [jnp.broadcast_to(note[:, 2:3], (8, width)) for note in notes]
    changes = []
    for s in range(slabs + 1):
        mode_x = jnp.where(
            rightward, 2 * slabs * (column - width // 2) + 2 * slabs - s, 2 * slabs * column + s
        )
        keep = jnp.where(mode_x == 0, 0.5, 1.0)
        if s in (0, slabs):
            keep = jnp.where(rightward, 0.0, keep)
        mode_x = mode_x.astype(F32)
        surpluses = []
        combined = None
        for g in range(groups):
            damping_x = 1.0 / (1.0 + (mode_x * factors_x[g]) ** 2)
            where = s * block + 8 * g
            surplus = damping_x * projected[where : where + 8] * dampings_v[g] * keep
            surpluses.append(surplus)
            part = weights[g] * surplus
            combined = part if combined is None else combined + part
        changes += [combined - surplus for surplus in surpluses]
    high, low = split(jnp.concatenate(changes, axis=0))
    waves[...] = dot(high, back_high[...]) + dot(low, back_high[...]) + dot(high, back_low[...])
    for g in range(groups):
        for j in range(parts):
            lanes = pl.ds(j * LANES, LANES)
            values = []
            for s in range(slabs + 1):
                where = pl.ds(s * block + 8 * g, 8)
                real, imag = waves[where, lanes], waves[where, pl.ds(slab_rows + j * LANES, LANES)]
                cosine, sine = twiddle[0, s, :, lanes], twiddle[1, s, :, lanes]
                if s == 0:
                    values.append((real, None))
                elif s == slabs:
                    values.append((real * cosine + imag * sine, None))
                else:
                    values.append((real * cosine + imag * sine, real * sine - imag * cosine))
            for d, value in enumerate(residues_to_slabs(values)):
                corrected[pl.ds(each * (g * slabs + d) + 8 * j, 8), :] = value
    lane = lax.broadcasted_iota(jnp.int32, (8, LANES), 1)
    for g in range(groups):
        for d in range(slabs):
            pieces = []
            for h, x in enumerate(halo_rows(slab_rows)):
                other = (d - 1) % slabs if x < 0 else (d + 1) % slabs
                at = packed_lane(slab_rows, x % slab_rows)
                source = corrected[pl.ds(each * (g * slabs + other) + at // LANES * 8, 8), :]
                pieces.append((source, at % LANES, h, 1))
            ends = jnp.where(lane < 2 * POST, moved_lanes(pieces), 0.0)
            ends = pltpu.roll(ends, 0, axis=1, stride=2 * POST, stride_axis=0)
            corrected[pl.ds(each * (g * slabs + d + 1) - 1, 1), :] = jnp.sum(ends, axis=0, keepdims=True)


def halo_rows(rows):
    return [x for x in range(-POST, 0)] + [rows + x for x in range(POST)]


def correct_kernel(
    levels, advanced, coef, parcels, bv_high, bv_low, result, first, second, work, natural, corrected, halo, sems, *, devices
):
    rows, width = result.shape
    planes = width // LANES
    _, _, diffusion = rates(levels)
    each, modes = parcel_rows(rows), bv_high.shape[1] // devices
    for q in range(devices):
        where = pl.ds(modes * q, modes)
        for j in range(rows // LANES):
            corrected[where, pl.ds(j * LANES, LANES)] = parcels[pl.ds(each * q + 8 * j, modes), :]
    ends = parcels[pl.ds(each - 1, devices, stride=each), :]
    for m in range(modes):
        shift = (LANES - 2 * POST * m) % LANES
        halo[pl.ds(m, devices, stride=modes), :] = pltpu.roll(ends, shift, axis=1) if shift else ends
    wide = []
    for t in range(PHASES):
        pieces = [
            (corrected[:, pl.ds(j * LANES, LANES)], packed, own, n) for j, b, packed, own, n in overlaps(rows) if b == t
        ]
        for h, x in enumerate(halo_rows(rows)):
            if (x + PHASES * MARGIN) % PHASES == t:
                pieces.append((halo[...], h, (x + PHASES * MARGIN) // PHASES, 1))
        wide.append(moved_lanes(pieces))
    high, low = split(jnp.concatenate(wide, axis=1))
    size = 2 * LANES
    chunks = width // size
    scale = diffusion * diffusion
    assert POST == 2
    copies = []
    stepped_to, plane = 0, 0
    for i in range(chunks + 2):
        if i > 1:
            ready = planes if i == chunks + 1 else (stepped_to - 1) // LANES
            while plane < ready:
                c = plane
                for k in range(LANES // 8):
                    values = stepped(second, coef, GUARD + c * LANES + 8 * k, 8, c < planes // 2)
                    for t, value in enumerate(values):
                        work[c % 2, t, pl.ds(8 * k, 8), :] = value * scale
                for t in range(PHASES):
                    back = work[c % 2, t].T
                    natural[c, pl.ds(t, rows // PHASES, stride=PHASES), :] = back[MARGIN : MARGIN + rows // PHASES]
                copies.append(
                    pltpu.make_async_copy(natural.at[c], result.at[:, pl.ds(c * LANES, LANES)], sems.at[0])
                )
                copies[-1].start()
                plane += 1
        if 0 < i <= chunks:
            if i == chunks:
                for t in range(PHASES):
                    first[t, pl.ds(GUARD + width, 1), :] = first[t, pl.ds(GUARD + width - 1, 1), :]
            last = width if i == chunks else i * size - 8
            for row in range(stepped_to, last, 8):
                for t, value in enumerate(stepped(first, coef, GUARD + row, 8, row < width // 2)):
                    second[t, pl.ds(GUARD + row, 8), :] = value
            if i == 1:
                for t in range(PHASES):
                    second[t, pl.ds(GUARD - 1, 1), :] = second[t, pl.ds(GUARD, 1), :]
            if i == chunks:
                for t in range(PHASES):
                    second[t, pl.ds(GUARD + width, 1), :] = second[t, pl.ds(GUARD + width - 1, 1), :]
            stepped_to = last
        if i < chunks:
            where = pl.ds(i * size, size)
            left_high, left_low = bv_high[where, :], bv_low[where, :]
            change = dot(left_high, high) + dot(left_high, low) + dot(left_low, high)
            for t in range(PHASES):
                lanes = slice(t * LANES, (t + 1) * LANES)
                first[t, pl.ds(GUARD + i * size, size), :] = advanced[t, where, :] + change[:, lanes]
            if i == 0:
                for t in range(PHASES):
                    first[t, pl.ds(GUARD - 1, 1), :] = first[t, pl.ds(GUARD, 1), :]
    for copy in copies:
        copy.wait()


def in_vmem(value):
    return pltpu.with_memory_space_constraint(value, pltpu.VMEM)


def in_hbm(value):
    return pltpu.with_memory_space_constraint(value, pltpu.HBM)


def body(densities, levels, coeffs):
    density = densities[0]
    rows, cells = density.shape
    groups, slabs = lax.axis_size("comp"), lax.axis_size("dom")
    devices = groups * slabs
    modes = MV // devices
    blocks = cells // LANES
    assert modes * devices == MV and modes <= 8 and slabs % 2 == 0 and blocks % 4 == 0 and MX % (2 * slabs) == 0

    table = cosine_table(cells, np.arange(MV), np.arange(cells))
    bv_high, bv_low = split_table(table)
    bvt_high, bvt_low = split_table(np.ascontiguousarray(table.T))
    packed = np.arange(rows)
    packed = PHASES * (packed % (rows // PHASES)) + packed // (rows // PHASES)
    ahead = residue_table(rows, slabs, packed)
    tables_x = [twiddle_table(rows, slabs, packed), *split_table(ahead), *split_table(np.ascontiguousarray(ahead.T))]

    vmem = pl.BlockSpec(memory_space=pltpu.VMEM)
    smem = pl.BlockSpec(memory_space=pltpu.SMEM)
    hbm = pl.BlockSpec(memory_space=pl.ANY)
    ring = [(i, (i + 1) % slabs) for i in range(slabs)]
    above = in_vmem(lax.ppermute(density[rows - HALO :], "dom", ring))
    below = in_vmem(lax.ppermute(density[:HALO], "dom", [(b, a) for a, b in ring]))

    assert rows % LANES == 0 and rows + HALO <= PHASES * (LANES - MARGIN) and PRE + POST <= HALO
    tall = pltpu.VMEM((PHASES, cells + 2 * GUARD, LANES), F32)
    flat = pltpu.VMEM((cells, PHASES * LANES), BF16)
    each = parcel_rows(rows)

    def exchange(parcels):
        flat_parcels = parcels.reshape(devices, 1, each * LANES)
        return in_vmem(lax.all_to_all(flat_parcels, AXES, 0, 0, tiled=True).reshape(devices * each, LANES))

    parcels_shape = pltpu.VMEM((devices * each, LANES), F32)
    limits = pltpu.CompilerParams(vmem_limit_bytes=VMEM_LIMIT)
    turned, coef = pl.pallas_call(
        turn_kernel,
        out_shape=(
            pltpu.VMEM((PHASES, cells, LANES), F32),
            pltpu.VMEM((2, cells + 2 * GUARD, LANES), F32),
        ),
        in_specs=[smem, hbm],
        out_specs=(vmem, vmem),
        scratch_shapes=[
            pltpu.VMEM((blocks, PHASES * LANES, LANES), F32),
            pltpu.SemaphoreType.DMA((blocks,)),
        ],
        compiler_params=limits,
        name="turn",
    )(in_hbm(levels), in_hbm(density))

    advanced, parcels = pl.pallas_call(
        functools.partial(advance_kernel, devices=devices, rows=rows),
        out_shape=(pltpu.VMEM((PHASES, cells, LANES), F32), parcels_shape),
        in_specs=[smem, smem, vmem, vmem, vmem, vmem, hbm, hbm],
        out_specs=(vmem, vmem),
        scratch_shapes=[
            tall,
            tall,
            pltpu.VMEM((blocks, 2 * HALO, LANES), F32),
            pltpu.VMEM((blocks, LANES, LANES), F32),
            flat,
            flat,
            pltpu.VMEM((MV, cells), BF16),
            pltpu.VMEM((MV, cells), BF16),
            pltpu.SemaphoreType.DMA((2,)),
        ],
        compiler_params=limits,
        name="advance",
    )(in_hbm(levels), coeffs, turned, coef, above, below, in_hbm(bvt_high), in_hbm(bvt_low))

    parcels = pl.pallas_call(
        functools.partial(combine_kernel, groups=groups, slabs=slabs, modes=modes),
        out_shape=parcels_shape,
        in_specs=[vmem] * 6,
        out_specs=vmem,
        scratch_shapes=[pltpu.VMEM((8 * groups * (slabs + 1), 2 * rows), F32)],
        compiler_params=limits,
        name="combine",
    )(exchange(parcels), *map(in_vmem, tables_x))

    result = pl.pallas_call(
        functools.partial(correct_kernel, devices=devices),
        out_shape=jax.ShapeDtypeStruct((rows, cells), F32),
        in_specs=[smem] + [vmem] * 5,
        out_specs=hbm,
        scratch_shapes=[
            tall,
            tall,
            pltpu.VMEM((2, PHASES, LANES, LANES), F32),
            pltpu.VMEM((blocks, rows, LANES), F32),
            pltpu.VMEM((MV, rows), F32),
            pltpu.VMEM((MV, LANES), F32),
            pltpu.SemaphoreType.DMA((1,)),
        ],
        compiler_params=limits,
        name="correct",
    )(in_hbm(levels), advanced, coef, exchange(parcels), in_vmem(bv_high), in_vmem(bv_low))
    return result[None]


def solution(mesh):
    placed = (P("comp", "dom", None), P("comp", None), P("comp"))
    return jax.shard_map(
        body, mesh=mesh, in_specs=placed, out_specs=P("comp", "dom", None), check_vma=False
    )
```

```python
import functools

import jax
import jax.numpy as jnp
import ml_dtypes
import numpy as np
from jax import lax
from jax.experimental import pallas as pl
from jax.experimental.pallas import tpu as pltpu
from jax.sharding import PartitionSpec as P

MX = 2048
MV = 256
PRE = 8
POST = 2
LANES = 128
HALO = 12
PHASES = 4
MARGIN = 8
GUARD = 8
VMEM_LIMIT = 32 * 2**20
AXES = ("comp", "dom")
F32 = jnp.float32
BF16 = jnp.bfloat16


def split_table(table):
    high = table.astype(ml_dtypes.bfloat16)
    low = (table - high.astype(np.float64)).astype(ml_dtypes.bfloat16)
    return high, low


def cosine_table(length, mode_ids, positions):
    scale = np.where(mode_ids == 0, np.sqrt(1.0 / length), np.sqrt(2.0 / length))
    turns = ((2 * positions[:, None] + 1) * mode_ids[None, :]) % (4 * length)
    return np.cos(np.pi * turns / (2.0 * length)) * scale[None, :]


def split(value):
    high = value.astype(BF16)
    return high, (value - high.astype(F32)).astype(BF16)


def dot(a, b, dims=((1,), (0,))):
    return lax.dot_general(a, b, (dims, ((), ())), preferred_element_type=F32)


def rates(levels_ref):
    level_x, level_v = levels_ref[0, 0], levels_ref[0, 1]
    courant = 0.3 + level_x.astype(F32) / 15.0
    diffusion = 0.1 + level_v.astype(F32) / 30.0
    return level_x, courant, diffusion


def fill_coefs(coef, cells, courant, diffusion):
    size = 128
    inverse = 1.0 / diffusion

    def rows(i, carry):
        at = (i * size + lax.broadcasted_iota(jnp.int32, (size, LANES), 0)).astype(F32)
        speed = courant * jnp.abs(-1.0 + (2.0 * at + 1.0) / cells)
        where = pl.ds(pl.multiple_of(GUARD + i * size, 8), size)
        coef[0, where, :] = (1.0 - speed - 2.0 * diffusion) * inverse
        coef[1, where, :] = speed * inverse
        return carry

    lax.fori_loop(0, cells // size, rows, 0)


def mirror_edges(buf, cells):
    for t in range(PHASES):
        buf[t, pl.ds(GUARD - 1, 1), :] = buf[t, pl.ds(GUARD, 1), :]
        buf[t, pl.ds(GUARD + cells, 1), :] = buf[t, pl.ds(GUARD + cells - 1, 1), :]


def stepped(src, coef, row, size, leftward):
    here = pl.ds(row, size)
    own, windward = coef[0, here, :], coef[1, here, :]
    cur = [src[t, here, :] for t in range(PHASES)]
    if leftward:
        wind = cur[1:] + [pltpu.roll(cur[0], LANES - 1, axis=1)]
    else:
        wind = [pltpu.roll(cur[-1], 1, axis=1)] + cur[:-1]
    return [
        own * cur[t]
        + windward * wind[t]
        + (src[t, pl.ds(row - 1, size), :] + src[t, pl.ds(row + 1, size), :])
        for t in range(PHASES)
    ]


def inner_step(src, dst, coef, cells):
    unroll = 64
    for leftward in (True, False):
        start = GUARD if leftward else GUARD + cells // 2

        def rows(i, carry):
            for k in range(unroll):
                row = pl.multiple_of(start + (i * unroll + k) * 8, 8)
                for t, value in enumerate(stepped(src, coef, row, 8, leftward)):
                    dst[t, pl.ds(row, 8), :] = value
            return carry

        lax.fori_loop(0, cells // 16 // unroll, rows, 0)
    mirror_edges(dst, cells)


def moved_lanes(pieces):
    out = None
    for source, origin, target, count in pieces:
        shift = (target - origin) % LANES
        moved = pltpu.roll(source, shift, axis=1) if shift else source
        if out is None:
            out = moved
        else:
            lane = lax.broadcasted_iota(jnp.int32, moved.shape, 1)
            out = jnp.where((lane >= target) & (lane < target + count), moved, out)
    return out


def overlaps(rows):
    quarter = rows // PHASES
    runs = []
    for j in range(rows // LANES):
        for t in range(PHASES):
            low, high = max(LANES * j, quarter * t), min(LANES * (j + 1), quarter * (t + 1))
            if low < high:
                runs.append((j, t, low - LANES * j, MARGIN + low - quarter * t, high - low))
    return runs


def parcel_rows(rows):
    return 8 * rows // LANES + 1


def packed_lane(rows, x):
    return (x % PHASES) * (rows // PHASES) + x // PHASES


def turn_kernel(levels, cells, turned, coef, natural, fetches):
    rows, width = cells.shape
    start = PHASES * MARGIN
    tail = start + rows
    copies = []
    for c in range(width // LANES):
        lanes = pl.ds(c * LANES, LANES)
        copies.append(
            pltpu.make_async_copy(cells.at[:, lanes], natural.at[c, pl.ds(start, rows), :], fetches.at[c])
        )
        copies[c].start()
    _, courant, diffusion = rates(levels)
    fill_coefs(coef, width, courant, diffusion)
    for c, copy in enumerate(copies):
        natural[c, pl.ds(0, start), :] = jnp.zeros((start, LANES), F32)
        natural[c, pl.ds(tail, PHASES * LANES - tail), :] = jnp.zeros((PHASES * LANES - tail, LANES), F32)
        copy.wait()
        for t in range(PHASES):
            turned[t, pl.ds(c * LANES, LANES), :] = natural[c, pl.ds(t, LANES, stride=PHASES), :].T


def advance_kernel(
    levels, coeffs, turned, coef, above, below, bvt_high_hbm, bvt_low_hbm, advanced, parcels,
    first, second, halos, strips, high, low, bvt_high, bvt_low, sems, *, devices, rows,
):
    width = turned.shape[1]
    planes = width // LANES
    tables = [
        pltpu.make_async_copy(bvt_high_hbm, bvt_high, sems.at[0]),
        pltpu.make_async_copy(bvt_low_hbm, bvt_low, sems.at[1]),
    ]
    for copy in tables:
        copy.start()
    level_x, _, diffusion = rates(levels)
    count = jnp.clip(PRE - 3 + level_x, 0, PRE)
    scale = lax.fori_loop(0, count, lambda i, s: s * diffusion, jnp.float32(1.0))
    run = HALO // PHASES
    sides = ((MARGIN - run, 0), (MARGIN + rows // PHASES, HALO))
    shift = 2 * run
    lane = lax.broadcasted_iota(jnp.int32, (LANES, LANES), 1)
    is_halo = jnp.zeros((LANES, LANES), jnp.bool_)
    for low_lane, _ in sides:
        is_halo = is_halo | ((lane >= low_lane) & (lane < low_lane + run))

    def insert(target):
        for c in range(planes):
            lanes = pl.ds(c * LANES, LANES)
            for a in range(run):
                halos[c, pl.ds(PHASES * a, PHASES), :] = above[a, :, lanes]
                halos[c, pl.ds(HALO + PHASES * a, PHASES), :] = below[a, :, lanes]
            for t in range(PHASES):
                for low_lane, row in sides:
                    at = (low_lane + shift * t) % LANES
                    strips[c, pl.ds(at, run), :] = halos[c, pl.ds(row + t, run, stride=PHASES), :]
            strip = strips[c].T
            where = pl.ds(c * LANES, LANES)
            for t in range(PHASES):
                moved = pltpu.roll(strip, LANES - shift * t, axis=1) if t else strip
                target[t, pl.ds(GUARD + c * LANES, LANES), :] = jnp.where(is_halo, moved, turned[t, where, :])
        mirror_edges(target, width)

    inner = count - 1

    @pl.when(inner % 2 == 0)
    def _():
        insert(first)

    @pl.when(inner % 2 == 1)
    def _():
        insert(second)
        inner_step(second, first, coef, width)

    def pair(i, carry):
        inner_step(first, second, coef, width)
        inner_step(second, first, coef, width)
        return carry

    lax.fori_loop(0, inner // 2, pair, 0)
    for copy in tables:
        copy.wait()
    size = 2 * LANES
    total = None
    for i in range(width // size + 1):
        if i < width // size:
            for k in range(size // 16):
                row = i * size + k * 16
                for t, value in enumerate(stepped(first, coef, GUARD + row, 16, row < width // 2)):
                    value = value * scale
                    advanced[t, pl.ds(row, 16), :] = value
                    lanes = pl.ds(t * LANES, LANES)
                    high[pl.ds(row, 16), lanes], low[pl.ds(row, 16), lanes] = split(value)
        if i > 0:
            where = pl.ds((i - 1) * size, size)
            left_high, left_low = bvt_high[:, where], bvt_low[:, where]
            right_high, right_low = high[where, :], low[where, :]
            part = dot(left_high, right_high) + dot(left_low, right_high) + dot(left_high, right_low)
            total = part if total is None else total + part
    modes = bvt_high.shape[0] // devices
    lane = lax.broadcasted_iota(jnp.int32, (1, LANES), 1)
    note = jnp.where(lane == 0, (1 << (3 - level_x)).astype(F32) / MX, 0.0)
    note = jnp.where(lane == 1, (1 << (3 - levels[0, 1])).astype(F32) / MV, note)
    note = jnp.where(lane == 2, coeffs[0].astype(F32), note)
    if modes < 8:
        parcels[...] = jnp.zeros_like(parcels)
    for j in range(rows // LANES):
        pieces = [
            (total[:, t * LANES : (t + 1) * LANES], own, packed, n) for b, t, packed, own, n in overlaps(rows) if b == j
        ]
        packed = moved_lanes(pieces)
        for q in range(devices):
            parcels[pl.ds(parcel_rows(rows) * q + 8 * j, modes), :] = packed[modes * q : modes * (q + 1)]
    for q in range(devices):
        parcels[pl.ds(parcel_rows(rows) * (q + 1) - 1, 1), :] = note


def rotate_sums(terms):
    total = None
    for factor, value in terms:
        if abs(factor) < 1e-12:
            continue
        if abs(factor - 1.0) < 1e-12:
            total = value if total is None else total + value
        elif abs(factor + 1.0) < 1e-12:
            total = -value if total is None else total - value
        else:
            part = value * np.float32(factor)
            total = part if total is None else total + part
    return total


def slab_angle(slabs, d, s):
    return np.cos(np.pi * d * s / slabs), np.sin(np.pi * d * s / slabs)


def slabs_to_residues(cells):
    slabs = len(cells)
    half = slabs // 2
    plus = {d: cells[d] + cells[slabs - d] for d in range(1, half)}
    minus = {d: cells[d] - cells[slabs - d] for d in range(1, half)}
    out = []
    for s in range(slabs + 1):
        same, other = (plus, minus) if s % 2 == 0 else (minus, plus)
        fixed = [(1.0, cells[0])], []
        middle = slab_angle(slabs, half, s)
        real = fixed[0] + [(middle[0], cells[half])] + [(slab_angle(slabs, d, s)[0], same[d]) for d in range(1, half)]
        imag = [(middle[1], cells[half])] + [(slab_angle(slabs, d, s)[1], other[d]) for d in range(1, half)]
        out.append((rotate_sums(real), rotate_sums(imag)))
    return out


def residues_to_slabs(values):
    slabs = len(values) - 1
    out = [None] * slabs
    for d in range(slabs // 2 + 1):
        first, second = [], []
        for s, (real, imag) in enumerate(values):
            cosine, sine = slab_angle(slabs, d, s)
            (first if s % 2 == 0 else second).append((cosine, real))
            if imag is not None:
                (second if s % 2 == 0 else first).append((-sine, imag))
        one, two = rotate_sums(first), rotate_sums(second)
        out[d] = one if two is None else one + two
        if 0 < d < slabs // 2:
            out[slabs - d] = one if two is None else one - two
    return out


def residue_table(rows, slabs, positions):
    used = MX // (2 * slabs)
    count = -(-used // LANES) * LANES
    q = np.arange(count)
    scale = np.where(q < used, np.sqrt(2.0 / (rows * slabs)), 0.0)[None, :]
    blocks = []
    for shift, sign in ((0, -1.0), (1, 1.0)):
        turns = ((2 * positions[:, None] + 1) * (q + shift)[None, :]) % (2 * rows)
        angle = np.pi * turns / rows
        blocks.append(np.concatenate([np.cos(angle) * scale, sign * np.sin(angle) * scale], axis=0))
    return np.concatenate(blocks, axis=1)


def twiddle_table(rows, slabs, positions):
    s = np.arange(slabs + 1)[:, None]
    angle = np.pi * ((2 * positions[None, :] + 1) * s) / (2.0 * rows * slabs)
    return np.stack([np.cos(angle), np.sin(angle)]).astype(np.float32)[:, :, None, :]


def combine_kernel(
    parcels, twiddle, ahead_high, ahead_low, back_high, back_low, corrected, waves, *, groups, slabs, modes
):
    slab_rows = twiddle.shape[3]
    parts = slab_rows // LANES
    each = parcel_rows(slab_rows)
    block = 8 * groups
    for g in range(groups):
        for j in range(parts):
            lanes = pl.ds(j * LANES, LANES)
            cells = [parcels[pl.ds(each * (g * slabs + d) + 8 * j, 8), :] for d in range(slabs)]
            for s, (real, imag) in enumerate(slabs_to_residues(cells)):
                where = pl.ds(s * block + 8 * g, 8)
                cosine, sine = twiddle[0, s, :, lanes], twiddle[1, s, :, lanes]
                if s == 0:
                    turned = real, jnp.zeros_like(real)
                elif imag is None:
                    turned = real * cosine, real * sine
                else:
                    turned = real * cosine - imag * sine, real * sine + imag * cosine
                waves[where, lanes] = turned[0]
                waves[where, pl.ds(slab_rows + j * LANES, LANES)] = turned[1]
    high, low = split(waves[...])
    projected = dot(high, ahead_high[...]) + dot(low, ahead_high[...]) + dot(high, ahead_low[...])
    width = projected.shape[1]
    own = lax.axis_index(AXES[0]) * slabs + lax.axis_index(AXES[1])
    row_mode = (own * modes + lax.broadcasted_iota(jnp.int32, (8, width), 0)).astype(F32)
    column = lax.broadcasted_iota(jnp.int32, (8, width), 1)
    rightward = column >= width // 2
    notes = [parcels[pl.ds(each * (g * slabs + 1) - 1, 1), :] for g in range(groups)]
    factors_x = [jnp.broadcast_to(note[:, 0:1], (8, width)) for note in notes]
    dampings_v = [1.0 / (1.0 + (row_mode * note[:, 1:2]) ** 2) for note in notes]
    weights = [jnp.broadcast_to(note[:, 2:3], (8, width)) for note in notes]
    changes = []
    for s in range(slabs + 1):
        mode_x = jnp.where(
            rightward, 2 * slabs * (column - width // 2) + 2 * slabs - s, 2 * slabs * column + s
        )
        keep = jnp.where(mode_x == 0, 0.5, 1.0)
        if s in (0, slabs):
            keep = jnp.where(rightward, 0.0, keep)
        mode_x = mode_x.astype(F32)
        surpluses = []
        combined = None
        for g in range(groups):
            damping_x = 1.0 / (1.0 + (mode_x * factors_x[g]) ** 2)
            where = s * block + 8 * g
            surplus = damping_x * projected[where : where + 8] * dampings_v[g] * keep
            surpluses.append(surplus)
            part = weights[g] * surplus
            combined = part if combined is None else combined + part
        changes += [combined - surplus for surplus in surpluses]
    high, low = split(jnp.concatenate(changes, axis=0))
    waves[...] = dot(high, back_high[...]) + dot(low, back_high[...]) + dot(high, back_low[...])
    for g in range(groups):
        for j in range(parts):
            lanes = pl.ds(j * LANES, LANES)
            values = []
            for s in range(slabs + 1):
                where = pl.ds(s * block + 8 * g, 8)
                real, imag = waves[where, lanes], waves[where, pl.ds(slab_rows + j * LANES, LANES)]
                cosine, sine = twiddle[0, s, :, lanes], twiddle[1, s, :, lanes]
                if s == 0:
                    values.append((real, None))
                elif s == slabs:
                    values.append((real * cosine + imag * sine, None))
                else:
                    values.append((real * cosine + imag * sine, real * sine - imag * cosine))
            for d, value in enumerate(residues_to_slabs(values)):
                corrected[pl.ds(each * (g * slabs + d) + 8 * j, 8), :] = value
    lane = lax.broadcasted_iota(jnp.int32, (8, LANES), 1)
    for g in range(groups):
        for d in range(slabs):
            pieces = []
            for h, x in enumerate(halo_rows(slab_rows)):
                other = (d - 1) % slabs if x < 0 else (d + 1) % slabs
                at = packed_lane(slab_rows, x % slab_rows)
                source = corrected[pl.ds(each * (g * slabs + other) + at // LANES * 8, 8), :]
                pieces.append((source, at % LANES, h, 1))
            ends = jnp.where(lane < 2 * POST, moved_lanes(pieces), 0.0)
            ends = pltpu.roll(ends, 0, axis=1, stride=2 * POST, stride_axis=0)
            corrected[pl.ds(each * (g * slabs + d + 1) - 1, 1), :] = jnp.sum(ends, axis=0, keepdims=True)


def halo_rows(rows):
    return [x for x in range(-POST, 0)] + [rows + x for x in range(POST)]


def correct_kernel(
    levels, advanced, coef, parcels, bv_high, bv_low, result, first, second, work, natural, corrected, halo, sems, *, devices
):
    rows, width = result.shape
    planes = width // LANES
    _, _, diffusion = rates(levels)
    each, modes = parcel_rows(rows), bv_high.shape[1] // devices
    for q in range(devices):
        where = pl.ds(modes * q, modes)
        for j in range(rows // LANES):
            corrected[where, pl.ds(j * LANES, LANES)] = parcels[pl.ds(each * q + 8 * j, modes), :]
    ends = parcels[pl.ds(each - 1, devices, stride=each), :]
    for m in range(modes):
        shift = (LANES - 2 * POST * m) % LANES
        halo[pl.ds(m, devices, stride=modes), :] = pltpu.roll(ends, shift, axis=1) if shift else ends
    wide = []
    for t in range(PHASES):
        pieces = [
            (corrected[:, pl.ds(j * LANES, LANES)], packed, own, n) for j, b, packed, own, n in overlaps(rows) if b == t
        ]
        for h, x in enumerate(halo_rows(rows)):
            if (x + PHASES * MARGIN) % PHASES == t:
                pieces.append((halo[...], h, (x + PHASES * MARGIN) // PHASES, 1))
        wide.append(moved_lanes(pieces))
    high, low = split(jnp.concatenate(wide, axis=1))
    size = 2 * LANES
    chunks = width // size
    scale = diffusion * diffusion
    assert POST == 2
    copies = []
    stepped_to, plane = 0, 0
    for i in range(chunks + 2):
        if i > 1:
            ready = planes if i == chunks + 1 else (stepped_to - 1) // LANES
            while plane < ready:
                c = plane
                for k in range(LANES // 8):
                    values = stepped(second, coef, GUARD + c * LANES + 8 * k, 8, c < planes // 2)
                    for t, value in enumerate(values):
                        work[c % 2, t, pl.ds(8 * k, 8), :] = value * scale
                for t in range(PHASES):
                    back = work[c % 2, t].T
                    natural[c, pl.ds(t, rows // PHASES, stride=PHASES), :] = back[MARGIN : MARGIN + rows // PHASES]
                copies.append(
                    pltpu.make_async_copy(natural.at[c], result.at[:, pl.ds(c * LANES, LANES)], sems.at[0])
                )
                copies[-1].start()
                plane += 1
        if 0 < i <= chunks:
            if i == chunks:
                for t in range(PHASES):
                    first[t, pl.ds(GUARD + width, 1), :] = first[t, pl.ds(GUARD + width - 1, 1), :]
            last = width if i == chunks else i * size - 8
            for row in range(stepped_to, last, 8):
                for t, value in enumerate(stepped(first, coef, GUARD + row, 8, row < width // 2)):
                    second[t, pl.ds(GUARD + row, 8), :] = value
            if i == 1:
                for t in range(PHASES):
                    second[t, pl.ds(GUARD - 1, 1), :] = second[t, pl.ds(GUARD, 1), :]
            if i == chunks:
                for t in range(PHASES):
                    second[t, pl.ds(GUARD + width, 1), :] = second[t, pl.ds(GUARD + width - 1, 1), :]
            stepped_to = last
        if i < chunks:
            where = pl.ds(i * size, size)
            left_high, left_low = bv_high[where, :], bv_low[where, :]
            change = dot(left_high, high) + dot(left_high, low) + dot(left_low, high)
            for t in range(PHASES):
                lanes = slice(t * LANES, (t + 1) * LANES)
                first[t, pl.ds(GUARD + i * size, size), :] = advanced[t, where, :] + change[:, lanes]
            if i == 0:
                for t in range(PHASES):
                    first[t, pl.ds(GUARD - 1, 1), :] = first[t, pl.ds(GUARD, 1), :]
    for copy in copies:
        copy.wait()


def in_vmem(value):
    return pltpu.with_memory_space_constraint(value, pltpu.VMEM)


def in_hbm(value):
    return pltpu.with_memory_space_constraint(value, pltpu.HBM)


def body(densities, levels, coeffs):
    density = densities[0]
    rows, cells = density.shape
    groups, slabs = lax.axis_size("comp"), lax.axis_size("dom")
    devices = groups * slabs
    modes = MV // devices
    blocks = cells // LANES
    assert modes * devices == MV and modes <= 8 and slabs % 2 == 0 and blocks % 4 == 0 and MX % (2 * slabs) == 0

    table = cosine_table(cells, np.arange(MV), np.arange(cells))
    bv_high, bv_low = split_table(table)
    bvt_high, bvt_low = split_table(np.ascontiguousarray(table.T))
    packed = np.arange(rows)
    packed = PHASES * (packed % (rows // PHASES)) + packed // (rows // PHASES)
    ahead = residue_table(rows, slabs, packed)
    tables_x = [twiddle_table(rows, slabs, packed), *split_table(ahead), *split_table(np.ascontiguousarray(ahead.T))]

    vmem = pl.BlockSpec(memory_space=pltpu.VMEM)
    smem = pl.BlockSpec(memory_space=pltpu.SMEM)
    hbm = pl.BlockSpec(memory_space=pl.ANY)
    ring = [(i, (i + 1) % slabs) for i in range(slabs)]
    tail = jnp.stack([density[at : at + PHASES] for at in range(rows - HALO, rows, PHASES)])
    head = jnp.stack([density[at : at + PHASES] for at in range(0, HALO, PHASES)])
    above = in_vmem(lax.ppermute(tail, "dom", ring))
    below = in_vmem(lax.ppermute(head, "dom", [(b, a) for a, b in ring]))

    assert rows % LANES == 0 and rows + HALO <= PHASES * (LANES - MARGIN) and PRE + POST <= HALO
    tall = pltpu.VMEM((PHASES, cells + 2 * GUARD, LANES), F32)
    flat = pltpu.VMEM((cells, PHASES * LANES), BF16)
    each = parcel_rows(rows)

    def exchange(parcels):
        flat_parcels = parcels.reshape(devices, 1, each * LANES)
        return in_vmem(lax.all_to_all(flat_parcels, AXES, 0, 0, tiled=True).reshape(devices * each, LANES))

    parcels_shape = pltpu.VMEM((devices * each, LANES), F32)
    limits = pltpu.CompilerParams(vmem_limit_bytes=VMEM_LIMIT)
    turned, coef = pl.pallas_call(
        turn_kernel,
        out_shape=(
            pltpu.VMEM((PHASES, cells, LANES), F32),
            pltpu.VMEM((2, cells + 2 * GUARD, LANES), F32),
        ),
        in_specs=[smem, hbm],
        out_specs=(vmem, vmem),
        scratch_shapes=[
            pltpu.VMEM((blocks, PHASES * LANES, LANES), F32),
            pltpu.SemaphoreType.DMA((blocks,)),
        ],
        compiler_params=limits,
        name="turn",
    )(in_hbm(levels), in_hbm(density))

    advanced, parcels = pl.pallas_call(
        functools.partial(advance_kernel, devices=devices, rows=rows),
        out_shape=(pltpu.VMEM((PHASES, cells, LANES), F32), parcels_shape),
        in_specs=[smem, smem, vmem, vmem, vmem, vmem, hbm, hbm],
        out_specs=(vmem, vmem),
        scratch_shapes=[
            tall,
            tall,
            pltpu.VMEM((blocks, 2 * HALO, LANES), F32),
            pltpu.VMEM((blocks, LANES, LANES), F32),
            flat,
            flat,
            pltpu.VMEM((MV, cells), BF16),
            pltpu.VMEM((MV, cells), BF16),
            pltpu.SemaphoreType.DMA((2,)),
        ],
        compiler_params=limits,
        name="advance",
    )(in_hbm(levels), coeffs, turned, coef, above, below, in_hbm(bvt_high), in_hbm(bvt_low))

    parcels = pl.pallas_call(
        functools.partial(combine_kernel, groups=groups, slabs=slabs, modes=modes),
        out_shape=parcels_shape,
        in_specs=[vmem] * 6,
        out_specs=vmem,
        scratch_shapes=[pltpu.VMEM((8 * groups * (slabs + 1), 2 * rows), F32)],
        compiler_params=limits,
        name="combine",
    )(exchange(parcels), *map(in_vmem, tables_x))

    result = pl.pallas_call(
        functools.partial(correct_kernel, devices=devices),
        out_shape=jax.ShapeDtypeStruct((rows, cells), F32),
        in_specs=[smem] + [vmem] * 5,
        out_specs=hbm,
        scratch_shapes=[
            tall,
            tall,
            pltpu.VMEM((2, PHASES, LANES, LANES), F32),
            pltpu.VMEM((blocks, rows, LANES), F32),
            pltpu.VMEM((MV, rows), F32),
            pltpu.VMEM((MV, LANES), F32),
            pltpu.SemaphoreType.DMA((1,)),
        ],
        compiler_params=limits,
        name="correct",
    )(in_hbm(levels), advanced, coef, exchange(parcels), in_vmem(bv_high), in_vmem(bv_low))
    return result[None]


def solution(mesh):
    placed = (P("comp", "dom", None), P("comp", None), P("comp"))
    return jax.shard_map(
        body, mesh=mesh, in_specs=placed, out_specs=P("comp", "dom", None), check_vma=False
    )
```

```python
import functools

import jax
import jax.numpy as jnp
import ml_dtypes
import numpy as np
from jax import lax
from jax.experimental import pallas as pl
from jax.experimental.pallas import tpu as pltpu
from jax.sharding import PartitionSpec as P

MX = 2048
MV = 256
PRE = 8
POST = 2
LANES = 128
HALO = 12
PHASES = 4
MARGIN = 8
GUARD = 8
VMEM_LIMIT = 32 * 2**20
AXES = ("comp", "dom")
F32 = jnp.float32
BF16 = jnp.bfloat16


def split_table(table):
    high = table.astype(ml_dtypes.bfloat16)
    low = (table - high.astype(np.float64)).astype(ml_dtypes.bfloat16)
    return high, low


def cosine_table(length, mode_ids, positions):
    scale = np.where(mode_ids == 0, np.sqrt(1.0 / length), np.sqrt(2.0 / length))
    turns = ((2 * positions[:, None] + 1) * mode_ids[None, :]) % (4 * length)
    return np.cos(np.pi * turns / (2.0 * length)) * scale[None, :]


def split(value):
    high = value.astype(BF16)
    return high, (value - high.astype(F32)).astype(BF16)


def dot(a, b, dims=((1,), (0,))):
    return lax.dot_general(a, b, (dims, ((), ())), preferred_element_type=F32)


def split_dot(high, low, right_high, right_low):
    half = high.shape[0] // 2
    parts = []
    for rows in (slice(0, half), slice(half, None)):
        parts.append(dot(high[rows], right_high) + dot(low[rows], right_high) + dot(high[rows], right_low))
    return jnp.concatenate(parts, axis=0)


def rates(levels_ref):
    level_x, level_v = levels_ref[0, 0], levels_ref[0, 1]
    courant = 0.3 + level_x.astype(F32) / 15.0
    diffusion = 0.1 + level_v.astype(F32) / 30.0
    return level_x, courant, diffusion


def fill_coefs(coef, cells, courant, diffusion):
    size = 128
    inverse = 1.0 / diffusion

    def rows(i, carry):
        at = (i * size + lax.broadcasted_iota(jnp.int32, (size, LANES), 0)).astype(F32)
        speed = courant * jnp.abs(-1.0 + (2.0 * at + 1.0) / cells)
        where = pl.ds(pl.multiple_of(GUARD + i * size, 8), size)
        coef[0, where, :] = (1.0 - speed - 2.0 * diffusion) * inverse
        coef[1, where, :] = speed * inverse
        return carry

    lax.fori_loop(0, cells // size, rows, 0)


def mirror_edges(buf, cells):
    for t in range(PHASES):
        buf[t, pl.ds(GUARD - 1, 1), :] = buf[t, pl.ds(GUARD, 1), :]
        buf[t, pl.ds(GUARD + cells, 1), :] = buf[t, pl.ds(GUARD + cells - 1, 1), :]


def stepped(src, coef, row, size, leftward):
    here = pl.ds(row, size)
    own, windward = coef[0, here, :], coef[1, here, :]
    cur = [src[t, here, :] for t in range(PHASES)]
    if leftward:
        wind = cur[1:] + [pltpu.roll(cur[0], LANES - 1, axis=1)]
    else:
        wind = [pltpu.roll(cur[-1], 1, axis=1)] + cur[:-1]
    return [
        own * cur[t]
        + windward * wind[t]
        + (src[t, pl.ds(row - 1, size), :] + src[t, pl.ds(row + 1, size), :])
        for t in range(PHASES)
    ]


def inner_step(src, dst, coef, cells):
    unroll = 64
    for leftward in (True, False):
        start = GUARD if leftward else GUARD + cells // 2

        def rows(i, carry):
            for k in range(unroll):
                row = pl.multiple_of(start + (i * unroll + k) * 8, 8)
                for t, value in enumerate(stepped(src, coef, row, 8, leftward)):
                    dst[t, pl.ds(row, 8), :] = value
            return carry

        lax.fori_loop(0, cells // 16 // unroll, rows, 0)
    mirror_edges(dst, cells)


def moved_lanes(pieces):
    out = None
    for source, origin, target, count in pieces:
        shift = (target - origin) % LANES
        moved = pltpu.roll(source, shift, axis=1) if shift else source
        if out is None:
            out = moved
        else:
            lane = lax.broadcasted_iota(jnp.int32, moved.shape, 1)
            out = jnp.where((lane >= target) & (lane < target + count), moved, out)
    return out


def overlaps(rows):
    quarter = rows // PHASES
    runs = []
    for j in range(rows // LANES):
        for t in range(PHASES):
            low, high = max(LANES * j, quarter * t), min(LANES * (j + 1), quarter * (t + 1))
            if low < high:
                runs.append((j, t, low - LANES * j, MARGIN + low - quarter * t, high - low))
    return runs


def parcel_rows(rows):
    return 8 * rows // LANES + 1


def packed_lane(rows, x):
    return (x % PHASES) * (rows // PHASES) + x // PHASES


def turn_kernel(levels, cells, turned, coef, natural, fetches):
    rows, width = cells.shape
    start = PHASES * MARGIN
    tail = start + rows
    copies = []
    for c in range(width // LANES):
        lanes = pl.ds(c * LANES, LANES)
        copies.append(
            pltpu.make_async_copy(cells.at[:, lanes], natural.at[c, pl.ds(start, rows), :], fetches.at[c])
        )
        copies[c].start()
    _, courant, diffusion = rates(levels)
    fill_coefs(coef, width, courant, diffusion)
    for c, copy in enumerate(copies):
        natural[c, pl.ds(0, start), :] = jnp.zeros((start, LANES), F32)
        natural[c, pl.ds(tail, PHASES * LANES - tail), :] = jnp.zeros((PHASES * LANES - tail, LANES), F32)
        copy.wait()
        for t in range(PHASES):
            turned[t, pl.ds(c * LANES, LANES), :] = natural[c, pl.ds(t, LANES, stride=PHASES), :].T


def advance_kernel(
    levels, coeffs, turned, coef, above, below, bvt_high_hbm, bvt_low_hbm, advanced, parcels,
    first, second, halos, strips, high, low, bvt_high, bvt_low, sems, *, devices, rows,
):
    width = turned.shape[1]
    planes = width // LANES
    tables = [
        pltpu.make_async_copy(bvt_high_hbm, bvt_high, sems.at[0]),
        pltpu.make_async_copy(bvt_low_hbm, bvt_low, sems.at[1]),
    ]
    for copy in tables:
        copy.start()
    level_x, _, diffusion = rates(levels)
    count = jnp.clip(PRE - 3 + level_x, 0, PRE)
    scale = lax.fori_loop(0, count, lambda i, s: s * diffusion, jnp.float32(1.0))
    run = HALO // PHASES
    sides = ((MARGIN - run, 0), (MARGIN + rows // PHASES, HALO))
    shift = 2 * run
    lane = lax.broadcasted_iota(jnp.int32, (LANES, LANES), 1)
    is_halo = jnp.zeros((LANES, LANES), jnp.bool_)
    for low_lane, _ in sides:
        is_halo = is_halo | ((lane >= low_lane) & (lane < low_lane + run))

    def insert(target):
        for c in range(planes):
            lanes = pl.ds(c * LANES, LANES)
            for a in range(run):
                halos[c, pl.ds(PHASES * a, PHASES), :] = above[a, :, lanes]
                halos[c, pl.ds(HALO + PHASES * a, PHASES), :] = below[a, :, lanes]
            for t in range(PHASES):
                for low_lane, row in sides:
                    at = (low_lane + shift * t) % LANES
                    strips[c, pl.ds(at, run), :] = halos[c, pl.ds(row + t, run, stride=PHASES), :]
            strip = strips[c].T
            where = pl.ds(c * LANES, LANES)
            for t in range(PHASES):
                moved = pltpu.roll(strip, LANES - shift * t, axis=1) if t else strip
                target[t, pl.ds(GUARD + c * LANES, LANES), :] = jnp.where(is_halo, moved, turned[t, where, :])
        mirror_edges(target, width)

    inner = count - 1

    @pl.when(inner % 2 == 0)
    def _():
        insert(first)

    @pl.when(inner % 2 == 1)
    def _():
        insert(second)
        inner_step(second, first, coef, width)

    def pair(i, carry):
        inner_step(first, second, coef, width)
        inner_step(second, first, coef, width)
        return carry

    lax.fori_loop(0, inner // 2, pair, 0)
    for copy in tables:
        copy.wait()
    size = 2 * LANES
    total = None
    for i in range(width // size + 1):
        if i < width // size:
            for k in range(size // 16):
                row = i * size + k * 16
                for t, value in enumerate(stepped(first, coef, GUARD + row, 16, row < width // 2)):
                    value = value * scale
                    advanced[t, pl.ds(row, 16), :] = value
                    lanes = pl.ds(t * LANES, LANES)
                    high[pl.ds(row, 16), lanes], low[pl.ds(row, 16), lanes] = split(value)
        if i > 0:
            where = pl.ds((i - 1) * size, size)
            left_high, left_low = bvt_high[:, where], bvt_low[:, where]
            right_high, right_low = high[where, :], low[where, :]
            part = dot(left_high, right_high) + dot(left_low, right_high) + dot(left_high, right_low)
            total = part if total is None else total + part
    modes = bvt_high.shape[0] // devices
    lane = lax.broadcasted_iota(jnp.int32, (1, LANES), 1)
    note = jnp.where(lane == 0, (1 << (3 - level_x)).astype(F32) / MX, 0.0)
    note = jnp.where(lane == 1, (1 << (3 - levels[0, 1])).astype(F32) / MV, note)
    note = jnp.where(lane == 2, coeffs[0].astype(F32), note)
    if modes < 8:
        parcels[...] = jnp.zeros_like(parcels)
    for j in range(rows // LANES):
        pieces = [
            (total[:, t * LANES : (t + 1) * LANES], own, packed, n) for b, t, packed, own, n in overlaps(rows) if b == j
        ]
        packed = moved_lanes(pieces)
        for q in range(devices):
            parcels[pl.ds(parcel_rows(rows) * q + 8 * j, modes), :] = packed[modes * q : modes * (q + 1)]
    for q in range(devices):
        parcels[pl.ds(parcel_rows(rows) * (q + 1) - 1, 1), :] = note


def rotate_sums(terms):
    total = None
    for factor, value in terms:
        if abs(factor) < 1e-12:
            continue
        if abs(factor - 1.0) < 1e-12:
            total = value if total is None else total + value
        elif abs(factor + 1.0) < 1e-12:
            total = -value if total is None else total - value
        else:
            part = value * np.float32(factor)
            total = part if total is None else total + part
    return total


def slab_angle(slabs, d, s):
    return np.cos(np.pi * d * s / slabs), np.sin(np.pi * d * s / slabs)


def slabs_to_residues(cells):
    slabs = len(cells)
    half = slabs // 2
    plus = {d: cells[d] + cells[slabs - d] for d in range(1, half)}
    minus = {d: cells[d] - cells[slabs - d] for d in range(1, half)}
    out = []
    for s in range(slabs + 1):
        same, other = (plus, minus) if s % 2 == 0 else (minus, plus)
        fixed = [(1.0, cells[0])], []
        middle = slab_angle(slabs, half, s)
        real = fixed[0] + [(middle[0], cells[half])] + [(slab_angle(slabs, d, s)[0], same[d]) for d in range(1, half)]
        imag = [(middle[1], cells[half])] + [(slab_angle(slabs, d, s)[1], other[d]) for d in range(1, half)]
        out.append((rotate_sums(real), rotate_sums(imag)))
    return out


def residues_to_slabs(values):
    slabs = len(values) - 1
    out = [None] * slabs
    for d in range(slabs // 2 + 1):
        first, second = [], []
        for s, (real, imag) in enumerate(values):
            cosine, sine = slab_angle(slabs, d, s)
            (first if s % 2 == 0 else second).append((cosine, real))
            if imag is not None:
                (second if s % 2 == 0 else first).append((-sine, imag))
        one, two = rotate_sums(first), rotate_sums(second)
        out[d] = one if two is None else one + two
        if 0 < d < slabs // 2:
            out[slabs - d] = one if two is None else one - two
    return out


def residue_table(rows, slabs, positions):
    used = MX // (2 * slabs)
    count = -(-used // LANES) * LANES
    q = np.arange(count)
    scale = np.where(q < used, np.sqrt(2.0 / (rows * slabs)), 0.0)[None, :]
    blocks = []
    for shift, sign in ((0, -1.0), (1, 1.0)):
        turns = ((2 * positions[:, None] + 1) * (q + shift)[None, :]) % (2 * rows)
        angle = np.pi * turns / rows
        blocks.append(np.concatenate([np.cos(angle) * scale, sign * np.sin(angle) * scale], axis=0))
    return np.concatenate(blocks, axis=1)


def twiddle_table(rows, slabs, positions):
    s = np.arange(slabs + 1)[:, None]
    angle = np.pi * ((2 * positions[None, :] + 1) * s) / (2.0 * rows * slabs)
    return np.stack([np.cos(angle), np.sin(angle)]).astype(np.float32)[:, :, None, :]


def combine_kernel(
    parcels, twiddle, ahead_high, ahead_low, back_high, back_low, corrected, waves, *, groups, slabs, modes
):
    slab_rows = twiddle.shape[3]
    parts = slab_rows // LANES
    each = parcel_rows(slab_rows)
    block = 8 * groups
    for g in range(groups):
        for j in range(parts):
            lanes = pl.ds(j * LANES, LANES)
            cells = [parcels[pl.ds(each * (g * slabs + d) + 8 * j, 8), :] for d in range(slabs)]
            for s, (real, imag) in enumerate(slabs_to_residues(cells)):
                where = pl.ds(s * block + 8 * g, 8)
                cosine, sine = twiddle[0, s, :, lanes], twiddle[1, s, :, lanes]
                if s == 0:
                    turned = real, jnp.zeros_like(real)
                elif imag is None:
                    turned = real * cosine, real * sine
                else:
                    turned = real * cosine - imag * sine, real * sine + imag * cosine
                waves[where, lanes] = turned[0]
                waves[where, pl.ds(slab_rows + j * LANES, LANES)] = turned[1]
    high, low = split(waves[...])
    projected = split_dot(high, low, ahead_high[...], ahead_low[...])
    width = projected.shape[1]
    own = lax.axis_index(AXES[0]) * slabs + lax.axis_index(AXES[1])
    row_mode = (own * modes + lax.broadcasted_iota(jnp.int32, (8, width), 0)).astype(F32)
    column = lax.broadcasted_iota(jnp.int32, (8, width), 1)
    rightward = column >= width // 2
    notes = [parcels[pl.ds(each * (g * slabs + 1) - 1, 1), :] for g in range(groups)]
    factors_x = [jnp.broadcast_to(note[:, 0:1], (8, width)) for note in notes]
    dampings_v = [1.0 / (1.0 + (row_mode * note[:, 1:2]) ** 2) for note in notes]
    weights = [jnp.broadcast_to(note[:, 2:3], (8, width)) for note in notes]
    changes = []
    for s in range(slabs + 1):
        mode_x = jnp.where(
            rightward, 2 * slabs * (column - width // 2) + 2 * slabs - s, 2 * slabs * column + s
        )
        keep = jnp.where(mode_x == 0, 0.5, 1.0)
        if s in (0, slabs):
            keep = jnp.where(rightward, 0.0, keep)
        mode_x = mode_x.astype(F32)
        surpluses = []
        combined = None
        for g in range(groups):
            damping_x = 1.0 / (1.0 + (mode_x * factors_x[g]) ** 2)
            where = s * block + 8 * g
            surplus = damping_x * projected[where : where + 8] * dampings_v[g] * keep
            surpluses.append(surplus)
            part = weights[g] * surplus
            combined = part if combined is None else combined + part
        changes += [combined - surplus for surplus in surpluses]
    high, low = split(jnp.concatenate(changes, axis=0))
    waves[...] = split_dot(high, low, back_high[...], back_low[...])
    for g in range(groups):
        for j in range(parts):
            lanes = pl.ds(j * LANES, LANES)
            values = []
            for s in range(slabs + 1):
                where = pl.ds(s * block + 8 * g, 8)
                real, imag = waves[where, lanes], waves[where, pl.ds(slab_rows + j * LANES, LANES)]
                cosine, sine = twiddle[0, s, :, lanes], twiddle[1, s, :, lanes]
                if s == 0:
                    values.append((real, None))
                elif s == slabs:
                    values.append((real * cosine + imag * sine, None))
                else:
                    values.append((real * cosine + imag * sine, real * sine - imag * cosine))
            for d, value in enumerate(residues_to_slabs(values)):
                corrected[pl.ds(each * (g * slabs + d) + 8 * j, 8), :] = value
    lane = lax.broadcasted_iota(jnp.int32, (8, LANES), 1)
    for g in range(groups):
        for d in range(slabs):
            pieces = []
            for h, x in enumerate(halo_rows(slab_rows)):
                other = (d - 1) % slabs if x < 0 else (d + 1) % slabs
                at = packed_lane(slab_rows, x % slab_rows)
                source = corrected[pl.ds(each * (g * slabs + other) + at // LANES * 8, 8), :]
                pieces.append((source, at % LANES, h, 1))
            ends = jnp.where(lane < 2 * POST, moved_lanes(pieces), 0.0)
            ends = pltpu.roll(ends, 0, axis=1, stride=2 * POST, stride_axis=0)
            corrected[pl.ds(each * (g * slabs + d + 1) - 1, 1), :] = jnp.sum(ends, axis=0, keepdims=True)


def halo_rows(rows):
    return [x for x in range(-POST, 0)] + [rows + x for x in range(POST)]


def correct_kernel(
    levels, advanced, coef, parcels, bv_high, bv_low, result, first, second, work, natural, corrected, halo, sems, *, devices
):
    rows, width = result.shape
    planes = width // LANES
    _, _, diffusion = rates(levels)
    each, modes = parcel_rows(rows), bv_high.shape[1] // devices
    for q in range(devices):
        where = pl.ds(modes * q, modes)
        for j in range(rows // LANES):
            corrected[where, pl.ds(j * LANES, LANES)] = parcels[pl.ds(each * q + 8 * j, modes), :]
    ends = parcels[pl.ds(each - 1, devices, stride=each), :]
    for m in range(modes):
        shift = (LANES - 2 * POST * m) % LANES
        halo[pl.ds(m, devices, stride=modes), :] = pltpu.roll(ends, shift, axis=1) if shift else ends
    wide = []
    for t in range(PHASES):
        pieces = [
            (corrected[:, pl.ds(j * LANES, LANES)], packed, own, n) for j, b, packed, own, n in overlaps(rows) if b == t
        ]
        for h, x in enumerate(halo_rows(rows)):
            if (x + PHASES * MARGIN) % PHASES == t:
                pieces.append((halo[...], h, (x + PHASES * MARGIN) // PHASES, 1))
        wide.append(moved_lanes(pieces))
    high, low = split(jnp.concatenate(wide, axis=1))
    size = 2 * LANES
    chunks = width // size
    scale = diffusion * diffusion
    assert POST == 2
    copies = []
    stepped_to, plane = 0, 0
    for i in range(chunks + 2):
        if i > 1:
            ready = planes if i == chunks + 1 else (stepped_to - 1) // LANES
            while plane < ready:
                c = plane
                for k in range(LANES // 8):
                    values = stepped(second, coef, GUARD + c * LANES + 8 * k, 8, c < planes // 2)
                    for t, value in enumerate(values):
                        work[c % 2, t, pl.ds(8 * k, 8), :] = value * scale
                for t in range(PHASES):
                    back = work[c % 2, t].T
                    natural[c, pl.ds(t, rows // PHASES, stride=PHASES), :] = back[MARGIN : MARGIN + rows // PHASES]
                copies.append(
                    pltpu.make_async_copy(natural.at[c], result.at[:, pl.ds(c * LANES, LANES)], sems.at[0])
                )
                copies[-1].start()
                plane += 1
        if 0 < i <= chunks:
            if i == chunks:
                for t in range(PHASES):
                    first[t, pl.ds(GUARD + width, 1), :] = first[t, pl.ds(GUARD + width - 1, 1), :]
            last = width if i == chunks else i * size - 8
            for row in range(stepped_to, last, 8):
                for t, value in enumerate(stepped(first, coef, GUARD + row, 8, row < width // 2)):
                    second[t, pl.ds(GUARD + row, 8), :] = value
            if i == 1:
                for t in range(PHASES):
                    second[t, pl.ds(GUARD - 1, 1), :] = second[t, pl.ds(GUARD, 1), :]
            if i == chunks:
                for t in range(PHASES):
                    second[t, pl.ds(GUARD + width, 1), :] = second[t, pl.ds(GUARD + width - 1, 1), :]
            stepped_to = last
        if i < chunks:
            where = pl.ds(i * size, size)
            left_high, left_low = bv_high[where, :], bv_low[where, :]
            change = dot(left_high, high) + dot(left_high, low) + dot(left_low, high)
            for t in range(PHASES):
                lanes = slice(t * LANES, (t + 1) * LANES)
                first[t, pl.ds(GUARD + i * size, size), :] = advanced[t, where, :] + change[:, lanes]
            if i == 0:
                for t in range(PHASES):
                    first[t, pl.ds(GUARD - 1, 1), :] = first[t, pl.ds(GUARD, 1), :]
    for copy in copies:
        copy.wait()


def in_vmem(value):
    return pltpu.with_memory_space_constraint(value, pltpu.VMEM)


def in_hbm(value):
    return pltpu.with_memory_space_constraint(value, pltpu.HBM)


def body(densities, levels, coeffs):
    density = densities[0]
    rows, cells = density.shape
    groups, slabs = lax.axis_size("comp"), lax.axis_size("dom")
    devices = groups * slabs
    modes = MV // devices
    blocks = cells // LANES
    assert modes * devices == MV and modes <= 8 and slabs % 2 == 0 and blocks % 4 == 0 and MX % (2 * slabs) == 0

    table = cosine_table(cells, np.arange(MV), np.arange(cells))
    bv_high, bv_low = split_table(table)
    bvt_high, bvt_low = split_table(np.ascontiguousarray(table.T))
    packed = np.arange(rows)
    packed = PHASES * (packed % (rows // PHASES)) + packed // (rows // PHASES)
    ahead = residue_table(rows, slabs, packed)
    tables_x = [twiddle_table(rows, slabs, packed), *split_table(ahead), *split_table(np.ascontiguousarray(ahead.T))]

    vmem = pl.BlockSpec(memory_space=pltpu.VMEM)
    smem = pl.BlockSpec(memory_space=pltpu.SMEM)
    hbm = pl.BlockSpec(memory_space=pl.ANY)
    ring = [(i, (i + 1) % slabs) for i in range(slabs)]
    tail = jnp.stack([density[at : at + PHASES] for at in range(rows - HALO, rows, PHASES)])
    head = jnp.stack([density[at : at + PHASES] for at in range(0, HALO, PHASES)])
    above = in_vmem(lax.ppermute(tail, "dom", ring))
    below = in_vmem(lax.ppermute(head, "dom", [(b, a) for a, b in ring]))

    assert rows % LANES == 0 and rows + HALO <= PHASES * (LANES - MARGIN) and PRE + POST <= HALO
    tall = pltpu.VMEM((PHASES, cells + 2 * GUARD, LANES), F32)
    flat = pltpu.VMEM((cells, PHASES * LANES), BF16)
    each = parcel_rows(rows)

    def exchange(parcels):
        flat_parcels = parcels.reshape(devices, 1, each * LANES)
        return in_vmem(lax.all_to_all(flat_parcels, AXES, 0, 0, tiled=True).reshape(devices * each, LANES))

    parcels_shape = pltpu.VMEM((devices * each, LANES), F32)
    limits = pltpu.CompilerParams(vmem_limit_bytes=VMEM_LIMIT)
    turned, coef = pl.pallas_call(
        turn_kernel,
        out_shape=(
            pltpu.VMEM((PHASES, cells, LANES), F32),
            pltpu.VMEM((2, cells + 2 * GUARD, LANES), F32),
        ),
        in_specs=[smem, hbm],
        out_specs=(vmem, vmem),
        scratch_shapes=[
            pltpu.VMEM((blocks, PHASES * LANES, LANES), F32),
            pltpu.SemaphoreType.DMA((blocks,)),
        ],
        compiler_params=limits,
        name="turn",
    )(in_hbm(levels), in_hbm(density))

    advanced, parcels = pl.pallas_call(
        functools.partial(advance_kernel, devices=devices, rows=rows),
        out_shape=(pltpu.VMEM((PHASES, cells, LANES), F32), parcels_shape),
        in_specs=[smem, smem, vmem, vmem, vmem, vmem, hbm, hbm],
        out_specs=(vmem, vmem),
        scratch_shapes=[
            tall,
            tall,
            pltpu.VMEM((blocks, 2 * HALO, LANES), F32),
            pltpu.VMEM((blocks, LANES, LANES), F32),
            flat,
            flat,
            pltpu.VMEM((MV, cells), BF16),
            pltpu.VMEM((MV, cells), BF16),
            pltpu.SemaphoreType.DMA((2,)),
        ],
        compiler_params=limits,
        name="advance",
    )(in_hbm(levels), coeffs, turned, coef, above, below, in_hbm(bvt_high), in_hbm(bvt_low))

    parcels = pl.pallas_call(
        functools.partial(combine_kernel, groups=groups, slabs=slabs, modes=modes),
        out_shape=parcels_shape,
        in_specs=[vmem] * 6,
        out_specs=vmem,
        scratch_shapes=[pltpu.VMEM((8 * groups * (slabs + 1), 2 * rows), F32)],
        compiler_params=limits,
        name="combine",
    )(exchange(parcels), *map(in_vmem, tables_x))

    result = pl.pallas_call(
        functools.partial(correct_kernel, devices=devices),
        out_shape=jax.ShapeDtypeStruct((rows, cells), F32),
        in_specs=[smem] + [vmem] * 5,
        out_specs=hbm,
        scratch_shapes=[
            tall,
            tall,
            pltpu.VMEM((2, PHASES, LANES, LANES), F32),
            pltpu.VMEM((blocks, rows, LANES), F32),
            pltpu.VMEM((MV, rows), F32),
            pltpu.VMEM((MV, LANES), F32),
            pltpu.SemaphoreType.DMA((1,)),
        ],
        compiler_params=limits,
        name="correct",
    )(in_hbm(levels), advanced, coef, exchange(parcels), in_vmem(bv_high), in_vmem(bv_low))
    return result[None]


def solution(mesh):
    placed = (P("comp", "dom", None), P("comp", None), P("comp"))
    return jax.shard_map(
        body, mesh=mesh, in_specs=placed, out_specs=P("comp", "dom", None), check_vma=False
    )
```
